32 devices in a mesh: dp: 16 (over z, y, x), mp: 2 (over core).
Axes of the slice: x: 2, y: 2, z: 4, core: 2. Of those that a mesh axis runs over, the one named last changes fastest.
Arguments:
- tokens: bfloat16 [32768, 384], P('dp'), may hold values from -6 to 6
- condition: bfloat16 [128, 384], P('dp'), may hold values from -6 to 6
- adaln_weight: bfloat16 [384, 2304], P('dp'), may hold values from -0.3125 to 0.3125
- adaln_bias: bfloat16 [6, 384], P(None, 'dp'), may hold values from -3 to 3
- qkv_weight: bfloat16 [3, 384, 384], P(None, 'dp', 'mp'), may hold values from -0.3125 to 0.3125
- qv_bias: bfloat16 [2, 2, 192], P(None, 'mp', 'dp'), may hold values from -3 to 3
- mix_weight: bfloat16 [384, 384], P('mp', 'dp'), may hold values from -1.25 to 1.25
- mix_bias: bfloat16 [384], P('dp'), may hold values from -3 to 3
- widen_weight: bfloat16 [384, 1536], P('dp', 'mp'), may hold values from -0.3125 to 0.3125
- widen_bias: bfloat16 [2, 768], P('mp', 'dp'), may hold values from -3 to 3
- narrow_weight: bfloat16 [1536, 384], P('mp', 'dp'), may hold values from -0.15625 to 0.15625
- narrow_bias: bfloat16 [384], P('dp'), may hold values from -3 to 3
- cotangent: bfloat16 [32768, 384], P('dp'), may hold values from -6 to 6
Outputs:
- block_out: bfloat16 [32768, 384], P('dp')
- tokens_grad: bfloat16 [32768, 384], P('dp')
- condition_grad: bfloat16 [128, 384], P('dp')
- adaln_weight_grad: float32 [384, 2304], P('dp')
- adaln_bias_grad: float32 [6, 384], P(None, 'dp')
- qkv_weight_grad: float32 [3, 384, 384], P(None, 'dp', 'mp')
- qv_bias_grad: float32 [2, 2, 192], P(None, 'mp', 'dp')
- mix_weight_grad: float32 [384, 384], P('mp', 'dp')
- mix_bias_grad: float32 [384], P('dp')
- expand_weight_grad: float32 [384, 1536], P('dp', 'mp')
- expand_bias_grad: float32 [2, 768], P('mp', 'dp')
- reduce_weight_grad: float32 [1536, 384], P('mp', 'dp')
- reduce_bias_grad: float32 [384], P('dp')
The draws below stay inside these ranges and needn't reach their ends.
All inputs are finite; a program needn't handle non-finite values.
Results may differ from the reference program's by a relative error of at most 0.015.
Values may be sent and summed in bfloat16 or wider, within the bound.
No kernel may reach another device: no remote copies, remote signals or barrier semaphores. Data moves between devices by JAX's collectives and lax.ppermute only.
A program may use at most 128 MiB of HBM per device.

```python
import math
import jax
import jax.numpy as jnp
from jax import lax

D = 384
HEADS = 6
HEAD_DIM = 64
FEEDFORWARD = 1536
S = 256
LATENTS = 128
TOKENS = 32768
N_MP = 2


def draw_condition(key, part):
    base = jax.random.normal(key, (LATENTS, D), jnp.float32)
    return jnp.clip(base, -6.0, 6.0).astype(jnp.bfloat16)


def spiked(drawn, own_key, source, target, parts, factor):
    def block_of(position):
        return (jnp.arange(drawn.shape[position]) // (drawn.shape[position] // parts)).reshape((-1,) + (1,) * (drawn.ndim - 1 - position))

    first = jax.random.permutation(own_key, parts)[block_of(target)]
    far = (block_of(target) + parts // 2) % parts
    return jnp.where((block_of(source) == first) | (block_of(source) == far), factor * drawn, drawn)


def block_levels(own_key, extent, cuts, least, top_value):
    level, own = 1.0, jax.random.fold_in(own_key, 6)
    for dim, parts in cuts:
        heights = jnp.exp(jax.random.uniform(jax.random.fold_in(own, dim), (parts,), jnp.float32, least / len(cuts), top_value / len(cuts)))
        level = level * jnp.repeat(heights, extent[dim] // parts).reshape([-1 if axis == dim else 1 for axis in range(len(extent))])
    return level


def normal_values(rng, extent, deviation, limit, shards=(), dtype=jnp.bfloat16):
    entries = jax.random.normal(rng, extent, jnp.float32) * deviation
    if len(shards) > 0:
        entries = block_levels(rng, extent, shards, -0.22, 0.18) * entries
    return jnp.clip(entries, min=-limit, max=limit).astype(dtype)


def bell_draw_with(key, dims, deviation, limit, split, heavy, dtype=jnp.bfloat16):
    drawn = deviation * jax.random.normal(key, dims, jnp.float32)
    if split:
        drawn = drawn * block_levels(key, dims, split, -0.22, 0.18)
    return jnp.clip(spiked(drawn, jax.random.fold_in(key, 3), *heavy), -limit, limit).astype(dtype)


def setup_inputs(seed: int = 0) -> dict:
    key_list = jax.random.split(jax.random.key(seed), 14)
    tokens = normal_values(key_list[0], (TOKENS, D), 1.0, 6.0, ((0, 16),))
    condition = draw_condition(jax.random.fold_in(key_list[13], 71), 0)
    adaln_weight = normal_values(key_list[2], (D, 6 * D), D ** -0.5, 0.3125, ((0, 16),))
    adaln_bias = normal_values(key_list[3], (6, D), 0.5, 3.0, ((1, 16),))
    qkv_weight = normal_values(key_list[4], (3, D, D), D ** -0.5, 0.3125, ((1, 16), (2, 2)))
    qv_bias = normal_values(key_list[5], (2, N_MP, D // N_MP), 0.5, 3.0, ((1, 2), (2, 16)))
    mix_weight = normal_values(key_list[6], (D, D), (D // 16) ** -0.5, 1.25, ((0, 2), (1, 16)))
    mix_bias = normal_values(key_list[7], (D,), 0.5, 3.0, ((0, 16),))
    widen_weight = normal_values(key_list[8], (D, FEEDFORWARD), D ** -0.5, 0.3125, ((0, 16), (1, 2)))
    widen_bias = normal_values(key_list[9], (N_MP, FEEDFORWARD // N_MP), 0.5, 3.0, ((0, 2), (1, 16)))
    narrow_weight = normal_values(key_list[10], (FEEDFORWARD, D), FEEDFORWARD ** -0.5, 0.15625, ((0, 2), (1, 16)))
    narrow_bias = normal_values(key_list[11], (D,), 0.5, 3.0, ((0, 16),))
    cotangent = bell_draw_with(key_list[12], (TOKENS, D), 1.0, 6.0, ((0, 16),), (0, 1, 16, 2.0))
    return dict(tokens=tokens, condition=condition, adaln_weight=adaln_weight, adaln_bias=adaln_bias, qkv_weight=qkv_weight, qv_bias=qv_bias, mix_weight=mix_weight, mix_bias=mix_bias, widen_weight=widen_weight, widen_bias=widen_bias, narrow_weight=narrow_weight, narrow_bias=narrow_bias, cotangent=cotangent)


EPS = 1e-06
HIGH_PRECISION = lax.Precision.HIGHEST

@jax.custom_vjp
def low(v):
    return lax.optimization_barrier(v.astype(jnp.bfloat16)).astype(jnp.float32)

@jax.custom_vjp
def lowered_backward(v):
    return v

def low_keep(v):
    return (low(v), None)

def low_pass(kept, grad):
    return (grad,)

def back_keep(v):
    return (v, None)

def back_low(kept, grad):
    return (low(grad),)
low.defvjp(low_keep, low_pass)
lowered_backward.defvjp(back_keep, back_low)

def silu_act(inputs):
    return inputs * jax.nn.sigmoid(inputs)

def gelu_tanh(inputs):
    return 0.5 * inputs * (1.0 + jnp.tanh(0.7978845608028654 * (inputs + 0.044715 * inputs * inputs * inputs)))

def normalize(inputs):
    centered = inputs - lax.optimization_barrier(jnp.mean(inputs, axis=-1, keepdims=True))
    return centered * lax.rsqrt(lax.optimization_barrier(jnp.mean(centered * centered, axis=-1, keepdims=True)) + EPS)

def modulate(inputs, shift, scale):
    return normalize(inputs) * (1.0 + scale) + shift

def block_forward(group_tokens, group_cond, adaln_weight, adaln_bias, qkv_weight, qv_bias, mix_weight, mix_bias, widen_weight, widen_bias, narrow_weight, narrow_bias):
    latents = group_cond.shape[0]
    cond_act = low(silu_act(group_cond))
    modulation = lowered_backward(jnp.dot(cond_act, adaln_weight, precision=HIGH_PRECISION) + adaln_bias.reshape(6 * D))
    pieces = modulation.reshape(latents, 6, 1, D)
    inputs = group_tokens.reshape(latents, S, D)
    normed_one = low(modulate(inputs, pieces[:, 0], pieces[:, 1]))
    flat_bias = qv_bias.reshape(2, D)
    bias_three = jnp.stack([flat_bias[0], jnp.zeros((D,), jnp.float32), flat_bias[1]])
    projected = jnp.einsum('lsd,jde->jlse', normed_one, qkv_weight, precision=HIGH_PRECISION) + bias_three[:, None, None, :]
    projected = lowered_backward(low(projected))
    head_view = projected.reshape(3, latents, S, HEADS, HEAD_DIM)
    scores = lowered_backward(jnp.einsum('lqhd,lkhd->lhqk', head_view[0], head_view[1], precision=HIGH_PRECISION) * HEAD_DIM ** (-0.5))
    exp_scores = jnp.exp(scores - lax.optimization_barrier(jnp.max(scores, axis=-1, keepdims=True)))
    attn_prob = exp_scores / lax.optimization_barrier(jnp.sum(exp_scores, axis=-1, keepdims=True))
    attended = jnp.einsum('lhqk,lkhd->lqhd', low(attn_prob), head_view[2], precision=HIGH_PRECISION)
    attended = lowered_backward(low(attended)).reshape(latents, S, D)
    attn_branch = lowered_backward(jnp.einsum('lse,ed->lsd', attended, mix_weight, precision=HIGH_PRECISION) + mix_bias)
    middle = inputs + pieces[:, 2] * attn_branch
    second_normed = low(modulate(middle, pieces[:, 3], pieces[:, 4]))
    before_activation = lowered_backward(jnp.einsum('ebc,cx->ebx', second_normed, widen_weight, precision=HIGH_PRECISION) + widen_bias.reshape(FEEDFORWARD))
    activated_hidden = low(gelu_tanh(before_activation))
    feedforward_branch = lowered_backward(jnp.einsum('qjb,be->qje', activated_hidden, narrow_weight, precision=HIGH_PRECISION) + narrow_bias)
    result = middle + pieces[:, 5] * feedforward_branch
    return result.reshape(latents * S, D)

def reference(tokens, condition, adaln_weight, adaln_bias, qkv_weight, qv_bias, mix_weight, mix_bias, widen_weight, widen_bias, narrow_weight, narrow_bias, cotangent):
    weights = tuple((item.astype(jnp.float32) for item in (adaln_weight, adaln_bias, qkv_weight, qv_bias, mix_weight, mix_bias, widen_weight, widen_bias, narrow_weight, narrow_bias)))
    per_group = math.gcd(LATENTS, max(1, 4096 // S))
    groups = LATENTS // per_group
    token_groups = tokens.astype(jnp.float32).reshape(groups, per_group * S, D)
    cond_groups = condition.astype(jnp.float32).reshape(groups, per_group, D)
    grad_groups = cotangent.astype(jnp.float32).reshape(groups, per_group * S, D)

    def one_group(totals, item):
        group_tokens, group_cond, group_grad = item
        result, backward = jax.vjp(block_forward, group_tokens, group_cond, *weights)
        grads = backward(group_grad)
        totals = tuple((left + right for left, right in zip(totals, grads[2:])))
        return (totals, (result, grads[0], grads[1]))
    start = tuple((jnp.zeros(item.shape, jnp.float32) for item in weights))
    totals, (results, token_grads, cond_grads) = lax.scan(one_group, start, (token_groups, cond_groups, grad_groups))
    block_out = results.reshape(TOKENS, D).astype(jnp.bfloat16)
    tokens_grad = token_grads.reshape(TOKENS, D).astype(jnp.bfloat16)
    condition_grad = cond_grads.reshape(LATENTS, D).astype(jnp.bfloat16)
    return (block_out, tokens_grad, condition_grad, totals[0], totals[1], totals[2], totals[3], totals[4], totals[5], totals[6], totals[7], totals[8], totals[9])
```

```python
import functools

import jax
import jax.numpy as jnp
from jax import lax
from jax.experimental import pallas as pl
from jax.experimental.pallas import tpu as pltpu
from jax.sharding import PartitionSpec as P

HEAD_DIM = 64
EPS = 1e-06
BF = jnp.bfloat16
F32 = jnp.float32
AXES = ("dp", "mp")
GELU_A = 0.7978845608028654
GELU_B = 0.044715


def nn(a, b):
    return lax.dot_general(a, b, (((1,), (0,)), ((), ())), preferred_element_type=F32)


def nt(a, b):
    return lax.dot_general(a, b, (((1,), (1,)), ((), ())), preferred_element_type=F32)


def wide(column, tokens):
    return jnp.concatenate([column] * (tokens // 128), axis=1)


def fold(array):
    total = array[:, :128]
    for at in range(128, array.shape[1], 128):
        total = total + array[:, at : at + 128]
    return total


def flipped(array):
    return array.astype(F32).T


def normalized(x):
    mean = jnp.mean(x, axis=0, keepdims=True)
    centered = x - mean
    inverse = lax.rsqrt(jnp.mean(centered * centered, axis=0, keepdims=True) + EPS)
    return centered * inverse, inverse


def norm_back(grad, normed, inverse):
    first = jnp.mean(grad, axis=0, keepdims=True)
    second = jnp.mean(grad * normed, axis=0, keepdims=True)
    return (grad - first - normed * second) * inverse


def bit_orders(bits):
    down = list(range(bits - 1, -1, -1))
    other = down[:-2] + [down[-1], down[-2]] if bits > 1 else down
    return down, other


def place_of(apart, core, bits):
    orders = bit_orders(bits)
    places = [
        sum(((apart >> b) & 1) << p for p, b in enumerate(order)) for order in orders
    ]
    return jnp.where(core == 0, places[0], places[1])


def hop_pairs(phase, bits, dp, mp):
    orders = bit_orders(bits)
    return [
        (d * mp + c, (d ^ (1 << orders[c % 2][phase])) * mp + c)
        for d in range(dp)
        for c in range(mp)
    ]


def core_pairs(dp, mp):
    return [(d * mp + c, d * mp + (c ^ 1)) for d in range(dp) for c in range(mp)]


def prep_kernel(dp, bits, rows, where, mine, other, adaln, qkv, qkv_t, mix_t, mix, widen,
                widen_t, narrow_t, narrow, bias):
    me, core = where[0], where[1]
    for ref, half in ((mine, core), (other, 1 - core)):
        for j in range(dp):
            at = place_of(me ^ j, core if ref is mine else 1 - core, bits)
            block = ref[at]
            keep = slice(j * rows, (j + 1) * rows)
            start = 0
            for out in (adaln, qkv, mix_t, widen, narrow_t, bias):
                width = out.shape[2]
                out[half, keep, :] = block[:, start : start + width]
                start += width
    for h in range(2):
        qkv_t[h] = flipped(qkv[h]).astype(BF)
        mix[h] = flipped(mix_t[h]).astype(BF)
        widen_t[h] = flipped(widen[h]).astype(BF)
        narrow[h] = flipped(narrow_t[h]).astype(BF)


def attention_kernel(where, tok, shift, scale, gate, qkv_t, qkv_bias, mix_t, mix_bias,
                     x1_o, att_o, qkv_o, prob_o, h1_o, abr_o):
    seq = tok.shape[0]
    x = flipped(tok[...])
    normed, _ = normalized(x)
    h1 = (normed * (1.0 + wide(scale[0], seq)) + wide(shift[0], seq)).astype(BF)
    h1_o[...] = h1
    third = qkv_t.shape[1] // 3
    heads = third // HEAD_DIM
    for h in range(2):
        part = nn(qkv_t[h], h1) + wide(qkv_bias[h], seq)
        qkv_o[h] = part.astype(BF)
    for h in range(2):
        for i in range(heads):
            base = i * HEAD_DIM
            q = qkv_o[h, base : base + HEAD_DIM, :]
            k = qkv_o[h, third + base : third + base + HEAD_DIM, :]
            v = qkv_o[h, 2 * third + base : 2 * third + base + HEAD_DIM, :]
            keys = flipped(k).astype(BF)
            scores = nn(keys, (q.astype(F32) * HEAD_DIM**-0.5).astype(BF))
            top = jnp.max(scores, axis=0, keepdims=True)
            raised = jnp.exp(scores - top)
            prob = (raised * (1.0 / jnp.sum(raised, axis=0, keepdims=True))).astype(BF)
            prob_o[h * heads + i] = prob
            att_o[h, base : base + HEAD_DIM, :] = nn(v, prob).astype(BF)
    abr = nn(mix_t[0], att_o[0]) + nn(mix_t[1], att_o[1]) + wide(mix_bias[...], seq)
    abr_o[...] = abr
    x1_o[...] = x + wide(gate[0], seq) * abr


def mlp_kernel(steps, dp, bits, where, x1_r, cot, shift, scale, gate, widen_t, widen_bias,
               narrow_t, narrow_bias, narrow, widen, out_o, dx1_o, dshift_o, dscale_o,
               dgate_o, nb_o, wb_o, w_grad, n_grad):
    step = pl.program_id(0)
    seq = cot.shape[0]

    @pl.when(step == 0)
    def _():
        nb_o[...] = jnp.zeros_like(nb_o)
        wb_o[...] = jnp.zeros_like(wb_o)
        w_grad[...] = jnp.zeros_like(w_grad)
        n_grad[...] = jnp.zeros_like(n_grad)

    x1 = x1_r[...]
    normed, inverse = normalized(x1)
    lift = 1.0 + wide(scale[0], seq)
    h2 = (normed * lift + wide(shift[0], seq)).astype(BF)
    dy = flipped(cot[...])
    gate_w = wide(gate[0], seq)
    dm = (gate_w * dy).astype(BF)
    nb_o[...] += fold(dm.astype(F32))
    hidden = widen_t.shape[1]
    chunk = 256 if hidden % 256 == 0 else hidden
    mbr = jnp.zeros(x1.shape, F32)
    dh2 = jnp.zeros(x1.shape, F32)
    for h in range(2):
        for at in range(0, hidden, chunk):
            cut = slice(at, at + chunk)
            u = nn(widen_t[h, cut, :], h2) + wide(widen_bias[h, cut, :], seq)
            squared = u * u
            bent = jnp.tanh(u * (GELU_A + (GELU_A * GELU_B) * squared))
            above = 1.0 + bent
            half_u = 0.5 * u
            g = (half_u * above).astype(BF)
            slope = 0.5 * above + half_u * (1.0 - bent * bent) * (
                GELU_A + (3.0 * GELU_A * GELU_B) * squared
            )
            dg = nn(narrow[h, cut, :], dm)
            du_f = dg * slope
            du = du_f.astype(BF)
            wb_o[h, cut, :] += fold(du.astype(F32))
            mbr = mbr + nn(narrow_t[h, :, cut], g)
            dh2 = dh2 + nn(widen[h, :, cut], du)
            n_grad[h, :, cut] += nt(dm, g)
            w_grad[h, :, cut] += nt(h2, du)
    mbr = mbr + wide(narrow_bias[...], seq)
    y = x1 + gate_w * mbr
    out_o[...] = y.T.astype(BF)
    dgate_o[0] = fold(dy * mbr)
    dshift_o[0] = fold(dh2)
    dscale_o[0] = fold(dh2 * normed)
    dx1_o[...] = dy + norm_back(dh2 * lift, normed, inverse)


def back_kernel(steps, dp, bits, where, tok, dx1_r, abr_r, att, qkv, prob_r, h1, shift, scale,
                gate, mix, qkv_w, tok_o, dshift_o, dscale_o, dgate_o, mb_o, qb_o, q_grad, m_grad,
                dqkv):
    step = pl.program_id(0)
    seq = tok.shape[0]

    @pl.when(step == 0)
    def _():
        mb_o[...] = jnp.zeros_like(mb_o)
        qb_o[...] = jnp.zeros_like(qb_o)
        q_grad[...] = jnp.zeros_like(q_grad)
        m_grad[...] = jnp.zeros_like(m_grad)

    dx1 = dx1_r[...]
    dgate_o[0] = fold(dx1 * abr_r[...])
    da = (wide(gate[0], seq) * dx1).astype(BF)
    mb_o[...] += fold(da.astype(F32))
    third = qkv.shape[1] // 3
    heads = third // HEAD_DIM
    for h in range(2):
        m_grad[h] += nt(da, att[h])
        datt = nn(mix[h], da).astype(BF)
        for i in range(heads):
            base = i * HEAD_DIM
            q = qkv[h, base : base + HEAD_DIM, :]
            k = qkv[h, third + base : third + base + HEAD_DIM, :]
            v = qkv[h, 2 * third + base : 2 * third + base + HEAD_DIM, :]
            prob = prob_r[h * heads + i]
            d_out = datt[base : base + HEAD_DIM, :]
            dprob = nn(flipped(v).astype(BF), d_out)
            prob_f = prob.astype(F32)
            weighted = prob_f * dprob
            inner = jnp.sum(weighted, axis=0, keepdims=True)
            dscores = (weighted - prob_f * inner).astype(BF)
            dq = (nn(k, dscores) * HEAD_DIM**-0.5).astype(BF)
            dk = (nt(q, dscores) * HEAD_DIM**-0.5).astype(BF)
            dv = nt(d_out, prob).astype(BF)
            dqkv[h, base : base + HEAD_DIM, :] = dq
            dqkv[h, third + base : third + base + HEAD_DIM, :] = dk
            dqkv[h, 2 * third + base : 2 * third + base + HEAD_DIM, :] = dv
    dh1 = nn(qkv_w[0], dqkv[0]) + nn(qkv_w[1], dqkv[1])
    for h in range(2):
        q_grad[h] += nt(h1[...], dqkv[h])
        qb_o[h] += fold(dqkv[h].astype(F32))
    x = flipped(tok[...])
    normed, inverse = normalized(x)
    dshift_o[0] = fold(dh1)
    dscale_o[0] = fold(dh1 * normed)
    grad = dx1 + norm_back(dh1 * (1.0 + wide(scale[0], seq)), normed, inverse)
    tok_o[...] = grad.T.astype(BF)


def full(shape):
    return pl.BlockSpec(shape, lambda *_: (0,) * len(shape))


def cost(flops, nbytes):
    return pl.CostEstimate(flops=int(flops), bytes_accessed=int(nbytes), transcendentals=0)


def run_prep(where, mine, other, half_widths, dp, bits, width):
    rows = width // dp
    n_adaln, n_qkv, n_mix, n_hidden, n_bias = half_widths
    shapes = [
        (2, width, n_adaln), (2, width, n_qkv), (2, n_qkv, width), (2, width, n_mix),
        (2, n_mix, width), (2, width, n_hidden), (2, n_hidden, width), (2, width, n_hidden),
        (2, n_hidden, width), (2, width, n_bias),
    ]
    return pl.pallas_call(
        functools.partial(prep_kernel, dp, bits, rows),
        out_shape=[jax.ShapeDtypeStruct(s, BF) for s in shapes],
        grid_spec=pltpu.PrefetchScalarGridSpec(
            num_scalar_prefetch=1, grid=(1,),
            in_specs=[full(mine.shape), full(other.shape)],
            out_specs=[full(s) for s in shapes],
        ),
        cost_estimate=cost(1e6, 2e7),
        name="prep",
    )(where, mine, other)


def rearranged(array, axes):
    return jnp.transpose(array, axes)


def body(
    tokens,
    condition,
    adaln_weight,
    adaln_bias,
    qkv_weight,
    qv_bias,
    mix_weight,
    mix_bias,
    widen_weight,
    widen_bias,
    narrow_weight,
    narrow_bias,
    cotangent,
):
    dp, mp = lax.axis_size("dp"), lax.axis_size("mp")
    bits = dp.bit_length() - 1
    me, core = lax.axis_index("dp"), lax.axis_index("mp")
    latents = condition.shape[0]
    own = latents // mp
    seq = tokens.shape[0] // latents
    width = tokens.shape[1]
    rows = width // dp
    n_third = qkv_weight.shape[2]
    n_hidden = widen_weight.shape[1]
    n_adaln = adaln_weight.shape[1] // mp
    where = jnp.stack([me, core]).astype(jnp.int32)

    bias_cols = jnp.concatenate(
        [adaln_bias.T, mix_bias[:, None], narrow_bias[:, None], qv_bias.reshape(rows, 1),
         widen_bias.reshape(rows, 2)], axis=1)
    n_bias = 128
    bias_cols = jnp.pad(bias_cols, ((0, 0), (0, n_bias - bias_cols.shape[1])))
    half = lax.dynamic_slice_in_dim(adaln_weight, core * n_adaln, n_adaln, axis=1)
    message = jnp.concatenate(
        [half, jnp.transpose(qkv_weight, (1, 0, 2)).reshape(rows, 3 * n_third), mix_weight.T,
         widen_weight, narrow_weight.T, bias_cols], axis=1)
    held = message[None]
    for phase in range(bits):
        came = lax.ppermute(held, AXES, hop_pairs(phase, bits, dp, mp))
        held = jnp.concatenate([held, came], axis=0)
    other = lax.ppermute(held, AXES, core_pairs(dp, mp))
    (adaln, qkv, qkv_t, mix_t, mix, widen, widen_t, narrow_t, narrow, bias) = run_prep(
        where, held, other, (n_adaln, 3 * n_third, n_third, n_hidden, n_bias), dp, bits, width)

    def spread(column):
        return jnp.broadcast_to(column[..., None], (*column.shape, 128)).astype(F32)

    bias = bias.astype(F32)
    qv = bias[:, :, 8].reshape(2, dp, 2, rows // 2)
    qv = jnp.moveaxis(qv, 2, 1).reshape(2, 2, n_third)
    qkv_bias = jnp.concatenate([qv[:, 0], jnp.zeros((2, n_third), F32), qv[:, 1]], axis=1)
    w_bias = bias[:, :, 9:11].reshape(2, n_hidden)

    cond_own = lax.dynamic_slice_in_dim(condition, core * own, own, axis=0).astype(F32)
    act = cond_own * jax.nn.sigmoid(cond_own)
    act_b = act.astype(BF)
    mod = jnp.concatenate(
        [jnp.dot(act_b, adaln[h], preferred_element_type=F32) for h in range(2)], axis=1)
    mod = mod.reshape(own, 6, width) + bias[0, :, :6].T[None]
    mods = [spread(mod[:, i]) for i in range(6)]

    T = own * seq
    tok_spec = pl.BlockSpec((seq, width), lambda i, w: (w[1] * own + i, 0))
    col = pl.BlockSpec((width, seq), lambda i, w: (0, i))
    mod_spec = pl.BlockSpec((1, width, 128), lambda i, w: (i, 0, 0))
    half_col = lambda n: pl.BlockSpec((2, n, seq), lambda i, w: (0, 0, i))
    heads = 2 * n_third // HEAD_DIM
    prob_spec = pl.BlockSpec((heads, seq, seq), lambda i, w: (i, 0, 0))
    flat = pl.BlockSpec((seq, width), lambda i, w: (i, 0))
    params = pltpu.CompilerParams(vmem_limit_bytes=60000 * 1024)

    x1, att, qkv_act, prob, h1, abr = pl.pallas_call(
        attention_kernel,
        out_shape=[
            jax.ShapeDtypeStruct((width, T), F32),
            jax.ShapeDtypeStruct((2, n_third, T), BF),
            jax.ShapeDtypeStruct((2, 3 * n_third, T), BF),
            jax.ShapeDtypeStruct((own * heads, seq, seq), BF),
            jax.ShapeDtypeStruct((width, T), BF),
            jax.ShapeDtypeStruct((width, T), F32),
        ],
        grid_spec=pltpu.PrefetchScalarGridSpec(
            num_scalar_prefetch=1, grid=(own,),
            in_specs=[tok_spec, mod_spec, mod_spec, mod_spec, full(qkv_t.shape),
                      full((2, 3 * n_third, 128)), full(mix_t.shape), full((width, 128))],
            out_specs=[col, half_col(n_third), half_col(3 * n_third), prob_spec, col, col],
        ),
        compiler_params=params,
        cost_estimate=cost(3e9, 2e7),
        name="attention",
    )(where, tokens, mods[0], mods[1], mods[2], qkv_t, spread(qkv_bias), mix_t,
      spread(bias[0, :, 6]))

    dmod_spec = mod_spec
    dmod_shape = jax.ShapeDtypeStruct((own, width, 128), F32)
    mlp_in = [x1, cotangent, mods[3], mods[4], mods[5], widen_t, spread(w_bias), narrow_t,
              spread(bias[0, :, 7]), narrow, widen]
    out_half, dx1, dshift2, dscale2, dgate2, nb, wb, w_grad, n_grad = pl.pallas_call(
        functools.partial(mlp_kernel, own, dp, bits),
        out_shape=[
            jax.ShapeDtypeStruct((T, width), BF),
            jax.ShapeDtypeStruct((width, T), F32),
            dmod_shape, dmod_shape, dmod_shape,
            jax.ShapeDtypeStruct((width, 128), F32),
            jax.ShapeDtypeStruct((2, n_hidden, 128), F32),
            jax.ShapeDtypeStruct(widen.shape, F32),
            jax.ShapeDtypeStruct(narrow_t.shape, F32),
        ],
        grid_spec=pltpu.PrefetchScalarGridSpec(
            num_scalar_prefetch=1, grid=(own,),
            in_specs=[col, tok_spec, mod_spec, mod_spec, mod_spec]
            + [full(a.shape) for a in mlp_in[5:]],
            out_specs=[flat, col, dmod_spec, dmod_spec, dmod_spec, full((width, 128)),
                       full((2, n_hidden, 128)), full(widen.shape), full(narrow_t.shape)],
        ),
        compiler_params=params,
        cost_estimate=cost(8e9, 2e7),
        name="mlp",
    )(where, *mlp_in)

    tok_half, dshift1, dscale1, dgate1, mb, qb, q_grad, m_grad = pl.pallas_call(
        functools.partial(back_kernel, own, dp, bits),
        out_shape=[
            jax.ShapeDtypeStruct((T, width), BF),
            dmod_shape, dmod_shape, dmod_shape,
            jax.ShapeDtypeStruct((width, 128), F32),
            jax.ShapeDtypeStruct((2, 3 * n_third, 128), F32),
            jax.ShapeDtypeStruct(qkv.shape, F32),
            jax.ShapeDtypeStruct(mix_t.shape, F32),
        ],
        grid_spec=pltpu.PrefetchScalarGridSpec(
            num_scalar_prefetch=1, grid=(own,),
            in_specs=[tok_spec, col, col, half_col(n_third), half_col(3 * n_third), prob_spec,
                      col, mod_spec, mod_spec, mod_spec, full(mix.shape), full(qkv.shape)],
            out_specs=[flat, dmod_spec, dmod_spec, dmod_spec, full((width, 128)),
                       full((2, 3 * n_third, 128)), full(qkv.shape), full(mix_t.shape)],
            scratch_shapes=[pltpu.VMEM((2, 3 * n_third, seq), BF)],
        ),
        compiler_params=params,
        cost_estimate=cost(6e9, 2e7),
        name="back",
    )(where, tokens, dx1, abr, att, qkv_act, prob, h1, mods[0], mods[1], mods[2], mix, qkv)

    def summed(a):
        return jnp.sum(a, axis=-1)

    mb, nb, qb, wb = summed(mb), summed(nb), summed(qb), summed(wb)
    qb = qb.reshape(2, 3, dp, rows // 2)
    qv_cols = jnp.stack([qb[:, 0], qb[:, 2]], axis=2).reshape(2, width)
    small = jnp.stack(
        [mb, nb, qv_cols[0], qv_cols[1]]
        + [wb.reshape(2, width, 2)[h, :, i] for h in range(2) for i in range(2)], axis=1)
    small = jnp.pad(small, ((0, 0), (0, 120)))
    parts = [
        jnp.concatenate([q_grad[h], m_grad[h], w_grad[h], n_grad[h], small], axis=1).astype(BF)
        for h in range(2)
    ]
    keep = jnp.where(core == 0, parts[0], parts[1])
    give = jnp.where(core == 0, parts[1], parts[0])
    got = lax.ppermute(give, AXES, core_pairs(dp, mp))
    both = keep.astype(F32) + got.astype(F32)
    blocks = both.reshape(dp, rows, -1)
    order = place_of(jnp.arange(dp) ^ me, core, bits)
    inverse = jnp.zeros((dp,), jnp.int32).at[order].set(jnp.arange(dp, dtype=jnp.int32))
    total = jnp.take(blocks, inverse, axis=0)
    for phase in reversed(range(bits)):
        n = total.shape[0] // 2
        came = lax.ppermute(total[n:].astype(BF), AXES, hop_pairs(phase, bits, dp, mp))
        total = total[:n] + came.astype(F32)
    total = total[0]
    cuts = [3 * n_third, 4 * n_third, 4 * n_third + n_hidden, 4 * n_third + 2 * n_hidden]
    q_own, m_own, w_own, n_own, s_own = jnp.split(total, cuts, axis=1)
    qkv_weight_grad = jnp.transpose(q_own.reshape(rows, 3, n_third), (1, 0, 2))
    mix_weight_grad = m_own.T
    narrow_weight_grad = n_own.T
    mix_bias_grad = s_own[:, 0]
    narrow_bias_grad = s_own[:, 1]
    qv_bias_grad = jnp.where(core == 0, s_own[:, 2], s_own[:, 3]).reshape(2, 1, rows // 2)
    widen_bias_grad = jnp.where(core == 0, s_own[:, 4:6], s_own[:, 6:8]).reshape(1, 2 * rows)

    dmod = jnp.stack(
        [summed(a) for a in (dshift1, dscale1, dgate1, dshift2, dscale2, dgate2)], axis=1)
    dmod = dmod.astype(BF).reshape(own, 2, 3 * width)
    dact = sum(
        jnp.einsum("le,de->ld", dmod[:, h], adaln[h], preferred_element_type=F32)
        for h in range(2))
    gate_s = jax.nn.sigmoid(cond_own)
    cond_own_grad = (dact * (gate_s + act * (1.0 - gate_s))).astype(BF)

    def joined(array):
        shape = (2 * array.shape[0], *array.shape[1:])
        came = lax.ppermute(array, AXES, core_pairs(dp, mp))
        n = array.shape[0]
        whole = jnp.zeros(shape, array.dtype)
        whole = lax.dynamic_update_slice_in_dim(whole, array, core * n, axis=0)
        return lax.dynamic_update_slice_in_dim(whole, came, (1 - core) * n, axis=0)

    condition_grad = joined(cond_own_grad)
    block_out = joined(out_half)
    tokens_grad = joined(tok_half)

    mine = jnp.where(core == 0, dmod[:, 0], dmod[:, 1])
    theirs = jnp.where(core == 0, dmod[:, 1], dmod[:, 0])
    came = lax.ppermute(theirs, AXES, core_pairs(dp, mp))
    first = jnp.where(core == 0, mine, came)
    second = jnp.where(core == 0, came, mine)
    cond_float = condition.astype(F32)
    act_all = (cond_float * jax.nn.sigmoid(cond_float)).astype(BF)
    held = jnp.concatenate(
        [jnp.concatenate([first, second], axis=0), act_all], axis=1)[None]
    for phase in range(bits):
        came = lax.ppermute(held, AXES, hop_pairs(phase, bits, dp, mp))
        held = jnp.concatenate([held, came], axis=0)
    held = held.reshape(dp * latents, -1)
    dmod_all, act_every = held[:, : 3 * width], held[:, 3 * width :]
    act_mine = lax.dynamic_slice_in_dim(act_every, me * rows, rows, axis=1)
    adaln_own = jnp.einsum("ld,le->de", act_mine, dmod_all, preferred_element_type=F32)
    bias_own = jnp.sum(dmod_all, axis=0, dtype=F32).reshape(3, width)
    bias_own = lax.dynamic_slice_in_dim(bias_own, me * rows, rows, axis=1)
    adaln_other = lax.ppermute(adaln_own, AXES, core_pairs(dp, mp))
    bias_other = lax.ppermute(bias_own, AXES, core_pairs(dp, mp))
    adaln_weight_grad = jnp.where(
        core == 0,
        jnp.concatenate([adaln_own, adaln_other], axis=1),
        jnp.concatenate([adaln_other, adaln_own], axis=1))
    adaln_bias_grad = jnp.where(
        core == 0,
        jnp.concatenate([bias_own, bias_other], axis=0),
        jnp.concatenate([bias_other, bias_own], axis=0))
    return (
        block_out,
        tokens_grad,
        condition_grad,
        adaln_weight_grad,
        adaln_bias_grad,
        qkv_weight_grad,
        qv_bias_grad,
        mix_weight_grad,
        mix_bias_grad,
        w_own,
        widen_bias_grad,
        narrow_weight_grad,
        narrow_bias_grad,
    )


def solution(mesh):
    return jax.shard_map(
        body,
        mesh=mesh,
        in_specs=(
            P("dp", None),
            P("dp", None),
            P("dp", None),
            P(None, "dp"),
            P(None, "dp", "mp"),
            P(None, "mp", "dp"),
            P("mp", "dp"),
            P("dp"),
            P("dp", "mp"),
            P("mp", "dp"),
            P("mp", "dp"),
            P("dp"),
            P("dp", None),
        ),
        out_specs=(
            P("dp", None),
            P("dp", None),
            P("dp", None),
            P("dp", None),
            P(None, "dp"),
            P(None, "dp", "mp"),
            P(None, "mp", "dp"),
            P("mp", "dp"),
            P("dp"),
            P("dp", "mp"),
            P("mp", "dp"),
            P("mp", "dp"),
            P("dp"),
        ),
        check_vma=False,
    )
```

```python
import functools

import jax
import jax.numpy as jnp
from jax import lax
from jax.experimental import pallas as pl
from jax.experimental.pallas import tpu as pltpu
from jax.sharding import PartitionSpec as P


HEAD_DIM = 64
EPS = 1e-06
BF = jnp.bfloat16
F32 = jnp.float32
AXES = ("dp", "mp")
GELU_A = 0.7978845608028654
GELU_B = 0.044715
BIAS = 64
LANES = 128
EXTRA = 16


def nn(a, b):
    return lax.dot_general(a, b, (((1,), (0,)), ((), ())), preferred_element_type=F32)


def nt(a, b):
    return lax.dot_general(a, b, (((1,), (1,)), ((), ())), preferred_element_type=F32)


def wide(column, tokens):
    return jnp.concatenate([column] * (tokens // LANES), axis=1)


def column_of(row):
    return jnp.broadcast_to(row, (LANES, row.shape[1])).T


def flipped(array):
    return array.astype(F32).T


def token_sum(array):
    return nt(jnp.ones((8, array.shape[1]), BF), array.astype(BF))


def normalized(x):
    mean = jnp.mean(x, axis=0, keepdims=True)
    centered = x - mean
    inverse = lax.rsqrt(jnp.mean(centered * centered, axis=0, keepdims=True) + EPS)
    return centered * inverse, inverse


def norm_back(grad, normed, inverse):
    first = jnp.mean(grad, axis=0, keepdims=True)
    second = jnp.mean(grad * normed, axis=0, keepdims=True)
    return (grad - first - normed * second) * inverse


def bit_orders(bits):
    down = list(range(bits - 1, -1, -1))
    other = down[:-2] + [down[-1], down[-2]] if bits > 1 else down
    return down, other


def place_of(apart, core, bits):
    orders = bit_orders(bits)
    places = [
        sum(((apart >> b) & 1) << p for p, b in enumerate(order)) for order in orders
    ]
    return jnp.where(core == 0, places[0], places[1])


def hop_pairs(phase, bits, dp, mp):
    orders = bit_orders(bits)
    return [
        (d * mp + c, (d ^ (1 << orders[c % 2][phase])) * mp + c)
        for d in range(dp)
        for c in range(mp)
    ]


def core_pairs(dp, mp):
    return [(d * mp + c, d * mp + (c ^ 1)) for d in range(dp) for c in range(mp)]


def pack_kernel(rows, adaln, adaln_b, qkv, qv_b, mix_t, mix_b, widen, widen_b, narrow_t,
                narrow_b, first_o, second_o, rows_s):
    core = lax.axis_index("mp")
    width = adaln.shape[1] // 6
    third, hidden = qkv.shape[2], widen.shape[1]
    half = rows // 2
    rows_s[...] = jnp.zeros_like(rows_s)
    rows_s[0:1, 0:half] = qv_b[0:1, :].astype(F32)
    rows_s[0:1, half:rows] = qv_b[1:2, :].astype(F32)
    rows_s[1:3, 0:rows] = adaln_b[0:2, :].astype(F32)
    rows_s[8:9, 0:rows] = widen_b[:, 0:rows].astype(F32)
    rows_s[9:10, 0:rows] = widen_b[:, rows : 2 * rows].astype(F32)
    rows_s[10:14, 0:rows] = adaln_b[2:6, :].astype(F32)
    rows_s[14:15, 0:rows] = mix_b[...].astype(F32)
    rows_s[15:16, 0:rows] = narrow_b[...].astype(F32)
    for out, at in ((first_o, 0), (second_o, 8)):
        turned = jnp.concatenate(
            [rows_s[at : at + 8, :], jnp.zeros((LANES - 8, LANES), F32)], axis=0).T
        out[:, out.shape[1] - BIAS :] = turned[0:rows, 0:BIAS].astype(BF)
    at = pl.multiple_of(core * width, LANES)
    first_o[:, 0:width] = adaln[:, pl.ds(at, width)]
    for j in range(3):
        first_o[:, width + j * third : width + (j + 1) * third] = qkv[j]
    at = pl.multiple_of((2 + 2 * core) * width, LANES)
    second_o[:, 0 : 2 * width] = adaln[:, pl.ds(at, 2 * width)]
    start = 2 * width
    second_o[:, start : start + hidden] = widen[...]
    second_o[:, start + hidden : start + 2 * hidden] = narrow_t[...]
    start += 2 * hidden
    second_o[:, start : start + third] = mix_t[...]


def gathered_blocks(where, dp, bits, mine, other):
    me, core = where[0], where[1]
    for parts, half in ((mine, core), (other, 1 - core)):
        for j in range(dp):
            at = place_of(me ^ j, half, bits)
            yield half, j, parts, at


def from_parts(parts, at, cut):
    low, high = parts
    count = low.shape[0]
    inside = lax.rem(at, count)
    return jnp.where(at < count, low[inside, :, cut], high[inside, :, cut])


def lane_only(block, lanes):
    keep = lax.broadcasted_iota(jnp.int32, block.shape, 1)
    return jnp.where(sum((keep == n).astype(jnp.int32) for n in lanes) > 0, block, 0.0)


def attention_kernel(dp, bits, rows, where, tok, cond, low, high, other_low, other_high,
                     att_o, qkv_o, prob_o, qkv_w_o, ada_o, mod_o,
                     qkv_t, bias_s, plain_s):
    step = pl.program_id(0)
    core = where[1]
    seq, width = tok.shape
    third = qkv_o.shape[1] // 3
    heads = third // HEAD_DIM
    ones = jnp.ones((EXTRA, seq), BF)

    @pl.when(step == 0)
    def _():
        plain_s[...] = jnp.zeros_like(plain_s)
        for half, j, parts, at in gathered_blocks(
                where, dp, bits, (low, high), (other_low, other_high)):
            keep = slice(j * rows, (j + 1) * rows)
            ada_o[half, keep, :] = from_parts(parts, at, slice(0, width))
            qkv_w_o[half, keep, :] = from_parts(parts, at, slice(width, width + 3 * third))
            bias = from_parts(parts, at, slice(width + 3 * third, width + 3 * third + BIAS))
            bias = bias.astype(F32)
            bias_s[keep, 0:BIAS] = bias
            column = lane_only(bias, (0,))
            n = rows // 2
            plain_s[half, j * n : (j + 1) * n, 0:BIAS] = column[0:n]
            plain_s[half, 2 * third + j * n : 2 * third + (j + 1) * n, 0:BIAS] = column[n:]
        bias_rows = bias_s[...].T
        act = cond[...].astype(F32)
        act = (act * jax.nn.sigmoid(act)).astype(BF)
        for h in range(2):
            qkv_t[h, :, 0:width] = flipped(qkv_w_o[h]).astype(BF)
            qkv_t[h, :, width:] = plain_s[h].astype(BF)
            mod_o[h] = nn(act, ada_o[h]) + bias_rows[1 + h : 2 + h, :]

    row = core * pl.num_programs(0) + step
    shift = column_of(mod_o[0, pl.ds(row, 1), :])
    lift = 1.0 + column_of(mod_o[1, pl.ds(row, 1), :])
    normed, _ = normalized(flipped(tok[...]))
    h1 = (normed * wide(lift, seq) + wide(shift, seq)).astype(BF)
    h1 = jnp.concatenate([h1, ones], axis=0)
    for h in range(2):
        qkv_o[h] = nn(qkv_t[h, :, 0 : width + EXTRA], h1).astype(BF)

    def scores_of(n):
        h, base = divmod(n, heads)
        base *= HEAD_DIM
        q = qkv_o[h, base : base + HEAD_DIM, :]
        k = qkv_o[h, third + base : third + base + HEAD_DIM, :]
        keys = flipped(k).astype(BF)
        return nn(keys, (q.astype(F32) * HEAD_DIM**-0.5).astype(BF))

    def finish(n, scores):
        h, base = divmod(n, heads)
        base *= HEAD_DIM
        v = qkv_o[h, 2 * third + base : 2 * third + base + HEAD_DIM, :]
        top = jnp.max(scores, axis=0, keepdims=True)
        raised = jnp.exp(scores - top)
        prob = (raised * (1.0 / jnp.sum(raised, axis=0, keepdims=True))).astype(BF)
        prob_o[n] = prob
        att_o[h, base : base + HEAD_DIM, :] = nn(v, prob).astype(BF)

    held = scores_of(0)
    for n in range(2 * heads):
        ahead = scores_of(n + 1) if n + 1 < 2 * heads else None
        finish(n, held)
        held = ahead


def put_blocks(dp, bits, where, outs, make):
    me, core = where[0], where[1]
    for out, half in zip(outs, (core, 1 - core)):
        for j in range(dp):
            out[place_of(me ^ j, half, bits)] = make(half, j).astype(BF)


def mlp_kernel(dp, bits, rows, where, tok, cot, att, cond, low, high, other_low, other_high,
               out_o, whole_o, datt_o, dx1_o, own_o, oth_o, own_d, oth_d, dact_o,
               widen_t, widen, narrow_t, narrow, mix_t, mix, ada, mods, bias_s, plain_s,
               w_acc, n_acc, m_acc, sums, dmods, g_s, du_s):
    step = pl.program_id(0)
    core = where[1]
    seq, width = cot.shape
    hidden = widen.shape[2]
    ones = jnp.ones((EXTRA, seq), BF)

    @pl.when(step == 0)
    def _():
        w_acc[...] = jnp.zeros_like(w_acc)
        n_acc[...] = jnp.zeros_like(n_acc)
        m_acc[...] = jnp.zeros_like(m_acc)
        sums[...] = jnp.zeros_like(sums)
        dmods[...] = jnp.zeros_like(dmods)
        plain_s[...] = jnp.zeros_like(plain_s)
        for half, j, parts, at in gathered_blocks(
                where, dp, bits, (low, high), (other_low, other_high)):
            keep = slice(j * rows, (j + 1) * rows)
            start = 0
            for ref in (ada, widen, narrow_t, mix_t):
                n = ref.shape[2]
                ref[half, keep, :] = from_parts(parts, at, slice(start, start + n))
                start += n
            bias = from_parts(parts, at, slice(start, start + BIAS)).astype(F32)
            bias_s[keep, 0:BIAS] = bias
            at = 2 * rows * j
            plain_s[half, at : at + rows, 0:BIAS] = lane_only(bias, (0,))
            plain_s[half, at + rows : at + 2 * rows, 0:BIAS] = lane_only(bias, (1,))
        bias_rows = bias_s[...].T
        act = cond[...].astype(F32)
        act = (act * jax.nn.sigmoid(act)).astype(BF)
        for h in range(2):
            widen_t[h, :, 0:width] = flipped(widen[h]).astype(BF)
            widen_t[h, :, width:] = plain_s[h].astype(BF)
            narrow[h] = flipped(narrow_t[h]).astype(BF)
            mix[h] = flipped(mix_t[h]).astype(BF)
            found = nn(act, ada[h])
            for p in range(2):
                n = 2 * h + p
                mods[n] = found[:, p * width : (p + 1) * width] + bias_rows[2 + n : 3 + n, :]

    row = core * pl.num_programs(0) + step
    gate1, shift2, scale2, gate2 = (
        wide(column_of(mods[n, pl.ds(row, 1), :]), seq) for n in range(4))
    abr = nn(mix_t[0], att[0]) + nn(mix_t[1], att[1])
    abr = abr + jnp.broadcast_to(bias_s[:, 6:7], abr.shape)
    x1 = flipped(tok[...]) + gate1 * abr
    normed, inverse = normalized(x1)
    lift = 1.0 + scale2
    h2 = (normed * lift + shift2).astype(BF)
    h2 = jnp.concatenate([h2, ones], axis=0)
    dy = flipped(cot[...])
    dm = (gate2 * dy).astype(BF)
    chunk = 256 if hidden % 256 == 0 else hidden
    cuts = [(h, slice(at, at + chunk)) for h in range(2) for at in range(0, hidden, chunk)]

    def grads(h, cut):
        n_acc[h, :, cut] += nt(dm, g_s[h, cut, :])
        w_acc[h, :, cut] += nt(h2[0 : width + 8], du_s[h, cut, :])

    def opened(h, cut):
        return nn(widen_t[h, cut, 0 : width + EXTRA], h2), nn(narrow[h, cut, :], dm)

    held = opened(*cuts[0])
    for n, (h, cut) in enumerate(cuts):
        u, dg = held
        if n + 1 < len(cuts):
            held = opened(*cuts[n + 1])
        if n > 0:
            grads(*cuts[n - 1])
        squared = u * u
        part = 0.5 * jnp.tanh(u * (GELU_A + (GELU_A * GELU_B) * squared)) + 0.5
        g = u * part
        slope = part + (g - g * part) * (2 * GELU_A + (6 * GELU_A * GELU_B) * squared)
        g_s[h, cut, :] = g.astype(BF)
        du_s[h, cut, :] = (dg * slope).astype(BF)
    grads(*cuts[-1])
    mbr = nn(narrow_t[0], g_s[0]) + nn(narrow_t[1], g_s[1])
    dh2 = nn(widen[0], du_s[0]) + nn(widen[1], du_s[1])
    mbr = mbr + jnp.broadcast_to(bias_s[:, 7:8], mbr.shape)
    y = (x1 + gate2 * mbr).T.astype(BF)
    out_o[...] = y
    whole_o[...] = y
    dx1 = dy + norm_back(dh2 * lift, normed, inverse)
    dx1_o[...] = dx1
    da = (gate1 * dx1).astype(BF)
    for h in range(2):
        m_acc[h] += nt(da, att[h])
        datt_o[h] = nn(mix[h], da).astype(BF)
    sums[0] += token_sum(da)
    sums[1] += token_sum(dm)
    for n, found in enumerate((dx1 * abr, dh2, dh2 * normed, dy * mbr)):
        dmods[n, pl.ds(row, 1), :] = token_sum(found)[0:1]

    @pl.when(step == pl.num_programs(0) - 1)
    def _():
        turned = [w_acc[h, width : width + 8, :].T for h in range(2)]
        flat = [sums[n].T for n in range(2)]
        for h in range(2):
            for j in range(dp):
                at = 2 * rows * j
                keep = slice(j * rows, (j + 1) * rows)
                cols = [flat[0][keep, 0:1], flat[1][keep, 0:1],
                        turned[h][at : at + rows, 0:1], turned[h][at + rows : at + 2 * rows, 0:1]]
                lane = lax.broadcasted_iota(jnp.int32, (rows, BIAS), 1)
                block = jnp.zeros((rows, BIAS), F32)
                for n, c in enumerate(cols):
                    block = jnp.where(lane == n, jnp.broadcast_to(c, block.shape), block)
                plain_s[h, keep, 0:BIAS] = block

        def make(half, j):
            keep = slice(j * rows, (j + 1) * rows)
            return jnp.concatenate(
                [w_acc[half, keep, :], n_acc[half, keep, :], m_acc[half, keep, :],
                 plain_s[half, keep, 0:BIAS]], axis=1)

        put_blocks(dp, bits, where, (own_o, oth_o), make)
        act = cond[...].astype(F32)
        act = act * jax.nn.sigmoid(act)
        mine = lax.broadcasted_iota(jnp.int32, act.shape, 0) // pl.num_programs(0) == core
        act = jnp.where(mine, act, 0.0).astype(BF)
        dact = jnp.zeros(act.shape, F32)
        for n in range(4):
            dact = dact + nt(dmods[n].astype(BF), ada[n // 2, :, (n % 2) * width : (n % 2 + 1) * width])
        dact_o[...] = dact
        for out, half in ((own_d, core), (oth_d, 1 - core)):
            for p in range(2):
                out[:, p * width : (p + 1) * width] = dmods[2 * half + p].astype(BF)
            out[:, 2 * width : 3 * width] = act


def back_kernel(dp, bits, rows, where, tok, cond, dx1_r, datt, qkv, prob_r, mods, qkv_w, ada,
                dact2, tok_o, whole_o, own_o, oth_o, rows_o, cond_o, q_acc, dmods, dqkv, plain_s):
    step = pl.program_id(0)
    core = where[1]
    seq, width = tok.shape
    third = qkv.shape[1] // 3
    heads = third // HEAD_DIM
    ones = jnp.ones((8, seq), BF)

    @pl.when(step == 0)
    def _():
        q_acc[...] = jnp.zeros_like(q_acc)
        dmods[...] = jnp.zeros_like(dmods)

    row = core * pl.num_programs(0) + step
    shift = wide(column_of(mods[0, pl.ds(row, 1), :]), seq)
    lift = 1.0 + wide(column_of(mods[1, pl.ds(row, 1), :]), seq)

    def dprob_of(n):
        h, base = divmod(n, heads)
        base *= HEAD_DIM
        v = qkv[h, 2 * third + base : 2 * third + base + HEAD_DIM, :]
        return nn(flipped(v).astype(BF), datt[h, base : base + HEAD_DIM, :])

    def finish(n, dprob):
        h, base = divmod(n, heads)
        base *= HEAD_DIM
        q = qkv[h, base : base + HEAD_DIM, :]
        k = qkv[h, third + base : third + base + HEAD_DIM, :]
        prob = prob_r[n]
        prob_f = prob.astype(F32)
        weighted = prob_f * dprob
        inner = jnp.sum(weighted, axis=0, keepdims=True)
        dscores = (weighted - prob_f * inner).astype(BF)
        dqkv[h, base : base + HEAD_DIM, :] = (nn(k, dscores) * HEAD_DIM**-0.5).astype(BF)
        dqkv[h, third + base : third + base + HEAD_DIM, :] = (
            nt(q, dscores) * HEAD_DIM**-0.5).astype(BF)
        dqkv[h, 2 * third + base : 2 * third + base + HEAD_DIM, :] = nt(
            datt[h, base : base + HEAD_DIM, :], prob).astype(BF)

    held = dprob_of(0)
    for n in range(2 * heads):
        ahead = dprob_of(n + 1) if n + 1 < 2 * heads else None
        finish(n, held)
        held = ahead
    normed, inverse = normalized(flipped(tok[...]))
    h1 = (normed * lift + shift).astype(BF)
    h1 = jnp.concatenate([h1, ones], axis=0)
    for h in range(2):
        q_acc[h] += nt(h1, dqkv[h])
    dh1 = nn(qkv_w[0], dqkv[0]) + nn(qkv_w[1], dqkv[1])
    grad = dx1_r[...] + norm_back(dh1 * lift, normed, inverse)
    grad = grad.T.astype(BF)
    tok_o[...] = grad
    whole_o[...] = grad
    for n, found in enumerate((dh1, dh1 * normed)):
        dmods[n, pl.ds(row, 1), :] = token_sum(found)[0:1]

    @pl.when(step == pl.num_programs(0) - 1)
    def _():
        n = rows // 2
        for h in range(2):
            turned = q_acc[h, width : width + 8, :].T
            for j in range(dp):
                for at, start in ((0, 0), (n, 2 * third)):
                    plain_s[h, j * rows + at : j * rows + at + n, :] = jnp.broadcast_to(
                        turned[start + j * n : start + (j + 1) * n, 0:1], (n, LANES))

        def make(half, j):
            keep = slice(j * rows, (j + 1) * rows)
            return jnp.concatenate(
                [q_acc[half, keep, :], plain_s[half, keep, 0:BIAS],
                 jnp.zeros((rows, own_o.shape[2] - 3 * third - BIAS), F32)], axis=1)

        put_blocks(dp, bits, where, (own_o, oth_o), make)
        c = cond[...].astype(F32)
        s = jax.nn.sigmoid(c)
        dact = dact2[...]
        for p in range(2):
            dact = dact + nt(dmods[p].astype(BF), ada[p])
        cond_o[...] = (dact * (s + c * s * (1.0 - s))).astype(BF)
        for p in range(2):
            rows_o[:, p * width : (p + 1) * width] = dmods[p].astype(BF)


def owned(me, rows, width):
    feature = lax.broadcasted_iota(jnp.int32, (width, LANES), 0)
    lane = lax.broadcasted_iota(jnp.int32, (width, LANES), 1)
    hit = jnp.where(lane < rows, (feature == rows * me + lane).astype(jnp.int32), 0)
    return hit.astype(F32).astype(BF)


def last_mlp_kernel(rows, width, where, kept, came, widen_o, narrow_o, mix_o, mix_b, narrow_b, widen_b,
                    ada_o, ada_b, act_o):
    hidden, third = widen_o.shape[1], mix_o.shape[1]
    total = kept[0:rows, :].astype(F32) + came[0:rows, :].astype(F32)
    widen_o[...] = total[:, 0:hidden]
    narrow_o[...] = total[:, hidden : 2 * hidden]
    mix_o[...] = total[:, 2 * hidden : 2 * hidden + third]
    small = total[:, 2 * hidden + third :].T
    mix_b[...] = small[0:1, :]
    narrow_b[...] = small[1:2, :]
    widen_b[:, 0:rows] = small[2:3, :]
    widen_b[:, rows : 2 * rows] = small[3:4, :]
    every = jnp.concatenate([kept[2 * rows :, 0 : 3 * width], came[rows:, 0 : 3 * width]], axis=0)
    pick = owned(where[0], rows, width)
    act = nn(every[:, 2 * width :], pick).T.astype(BF)
    act_o[...] = act
    ada_o[...] = nn(act, every[:, 0 : 2 * width])[0:rows]
    ada_b[...] = jnp.zeros_like(ada_b)
    for p in range(2):
        found = nn(every[:, p * width : (p + 1) * width], pick)
        ada_b[p : p + 1, :] = jnp.sum(found, axis=0, keepdims=True)


def last_back_kernel(rows, width, where, kept, came, act, early, early_other, early_b,
                     early_other_b, qkv_o, qv_b, ada_o, ada_b):
    third = qkv_o.shape[2]
    core = where[1]
    total = kept[0:rows, :].astype(F32) + came[0:rows, :].astype(F32)
    for j in range(3):
        qkv_o[j] = total[:, j * third : (j + 1) * third]
    small = total[:, 3 * third : 3 * third + BIAS].T
    n = rows // 2
    qv_b[0:1, :] = small[0:1, 0:n]
    qv_b[1:2, :] = small[0:1, n:rows]
    every = jnp.concatenate([kept[2 * rows :, :], came[rows:, :]], axis=0)
    ada_o[:, 0 : 2 * width] = nn(act[...], every)[0:rows]
    pick = owned(where[0], rows, width)
    for p in range(2):
        found = nn(every[:, p * width : (p + 1) * width], pick)
        ada_b[p : p + 1, :] = jnp.sum(found, axis=0, keepdims=True)[:, 0:rows]
    for half, values in ((core, early), (1 - core, early_other)):
        at = pl.multiple_of((2 + 2 * half) * width, LANES)
        ada_o[:, pl.ds(at, 2 * width)] = values[...]
    first = jnp.where(core == 0, early_b[...], early_other_b[...])
    second = jnp.where(core == 0, early_other_b[...], early_b[...])
    ada_b[2:4, :] = first[0:2, 0:rows]
    ada_b[4:6, :] = second[0:2, 0:rows]


def full(shape):
    return pl.BlockSpec(tuple(shape), lambda *_: (0,) * len(shape))


def cost(flops, nbytes):
    return pl.CostEstimate(flops=int(flops), bytes_accessed=int(nbytes), transcendentals=0)


PARAMS = pltpu.CompilerParams(vmem_limit_bytes=58 * 1024 * 1024)


def local_call(kernel, where, args, in_specs, outs, out_specs, scratch=(), grid=(1,), price=(1e6, 4e6)):
    return pl.pallas_call(
        kernel,
        out_shape=[jax.ShapeDtypeStruct(tuple(s), d) for s, d in outs],
        grid_spec=pltpu.PrefetchScalarGridSpec(
            num_scalar_prefetch=1, grid=grid, in_specs=in_specs, out_specs=out_specs,
            scratch_shapes=list(scratch)),
        compiler_params=PARAMS,
        cost_estimate=cost(*price),
    )(where, *args)


def plain_call(kernel, args, outs, scratch=()):
    return pl.pallas_call(
        kernel,
        out_shape=[jax.ShapeDtypeStruct(tuple(s), d) for s, d in outs],
        in_specs=[pl.BlockSpec(memory_space=pltpu.VMEM)] * len(args),
        out_specs=[pl.BlockSpec(memory_space=pltpu.VMEM)] * len(outs),
        scratch_shapes=list(scratch),
        compiler_params=PARAMS,
        cost_estimate=cost(1e6, 1e6),
    )(*args)


def whole_call(kernel, where, args, outs, scratch=()):
    return local_call(kernel, where, args, [full(a.shape) for a in args], outs,
                      [full(s) for s, _ in outs], scratch)


def hop(array, pairs):
    return lax.ppermute(array, AXES, pairs)


def gathered(message, bits, dp, mp):
    held = message[None]
    came = None
    for phase in range(bits):
        if came is not None:
            held = jnp.concatenate([held, came], axis=0)
        came = hop(held, hop_pairs(phase, bits, dp, mp))
    pairs = core_pairs(dp, mp)
    return held, came, hop(held, pairs), hop(came, pairs)


def reduced(own, other, own_rows, other_rows, bits, dp, mp):
    rows, wide_by = own.shape[1:]
    pairs = core_pairs(dp, mp)
    got = hop(other, pairs)
    got_rows = hop(other_rows, pairs)
    blocks = (own.astype(F32) + got.astype(F32)).astype(BF).reshape(dp * rows, wide_by)
    extra = (own_rows.astype(F32) + got_rows.astype(F32)).astype(BF)
    if extra.shape[1] < wide_by:
        extra = jnp.pad(extra, ((0, 0), (0, wide_by - extra.shape[1])))
    held = jnp.concatenate([blocks, extra], axis=0)
    for phase in reversed(range(bits)):
        n = (1 << phase) * rows
        came = hop(held[n:], hop_pairs(phase, bits, dp, mp))
        if phase:
            added = (held[:n].astype(F32) + came[:n].astype(F32)).astype(BF)
            held = jnp.concatenate([added, held[2 * n :], came[n:]], axis=0)
    return held, came


def body(
    tokens,
    condition,
    adaln_weight,
    adaln_bias,
    qkv_weight,
    qv_bias,
    mix_weight,
    mix_bias,
    widen_weight,
    widen_bias,
    narrow_weight,
    narrow_bias,
    cotangent,
):
    dp, mp = lax.axis_size("dp"), lax.axis_size("mp")
    bits = dp.bit_length() - 1
    me, core = lax.axis_index("dp"), lax.axis_index("mp")
    latents = condition.shape[0]
    own = latents // mp
    seq = tokens.shape[0] // latents
    width = tokens.shape[1]
    rows = width // dp
    third = qkv_weight.shape[2]
    hidden = widen_weight.shape[1]
    where = jnp.stack([me, core]).astype(jnp.int32)
    T = own * seq
    heads = 2 * third // HEAD_DIM

    first_width = width + 3 * third + BIAS
    second_width = 2 * width + 2 * hidden + third + BIAS
    first, second = plain_call(
        functools.partial(pack_kernel, rows),
        [adaln_weight, adaln_bias, qkv_weight, qv_bias.reshape(2, rows // 2), mix_weight.T,
         mix_bias.reshape(1, rows), widen_weight, widen_bias, narrow_weight.T,
         narrow_bias.reshape(1, rows)],
        [((rows, first_width), BF), ((rows, second_width), BF)],
        [pltpu.VMEM((16, LANES), F32)])

    part_a = gathered(first, bits, dp, mp)
    part_b = gathered(second, bits, dp, mp)

    tok_spec = pl.BlockSpec((seq, width), lambda i, w: (w[1] * own + i, 0))
    col = pl.BlockSpec((width, seq), lambda i, w: (0, i))
    half_col = lambda n: pl.BlockSpec((2, n, seq), lambda i, w: (0, 0, i))
    prob_spec = pl.BlockSpec((heads, seq, seq), lambda i, w: (i, 0, 0))
    flat = pl.BlockSpec((seq, width), lambda i, w: (i, 0))

    def fulls(arrays):
        return [full(a.shape) for a in arrays]

    att, qkv_act, prob, qkv_w, ada1, mods1 = local_call(
        functools.partial(attention_kernel, dp, bits, rows), where,
        [tokens, condition, *part_a],
        [tok_spec, full(condition.shape), *fulls(part_a)],
        [((2, third, T), BF), ((2, 3 * third, T), BF), ((own * heads, seq, seq), BF),
         ((2, width, 3 * third), BF), ((2, width, width), BF), ((2, latents, width), F32)],
        [half_col(third), half_col(3 * third), prob_spec, full((2, width, 3 * third)),
         full((2, width, width)), full((2, latents, width))],
        [pltpu.VMEM((2, 3 * third, width + LANES), BF), pltpu.VMEM((width, LANES), F32),
         pltpu.VMEM((2, 3 * third, LANES), F32)],
        grid=(own,), price=(3e9, 2e7))

    send_width = 2 * hidden + third + BIAS
    out_half, out_whole, datt, dx1, own_m, oth_m, own_md, oth_md, dact2 = local_call(
        functools.partial(mlp_kernel, dp, bits, rows), where,
        [tokens, cotangent, att, condition, *part_b],
        [tok_spec, tok_spec, half_col(third), full(condition.shape), *fulls(part_b)],
        [((T, width), BF), (tokens.shape, BF), ((2, third, T), BF), ((width, T), F32),
         ((dp, rows, send_width), BF), ((dp, rows, send_width), BF),
         ((latents, 3 * width), BF), ((latents, 3 * width), BF), ((latents, width), F32)],
        [flat, tok_spec, half_col(third), col, full((dp, rows, send_width)),
         full((dp, rows, send_width)), full((latents, 3 * width)), full((latents, 3 * width)),
         full((latents, width))],
        [pltpu.VMEM((2, hidden, width + LANES), BF), pltpu.VMEM((2, width, hidden), BF),
         pltpu.VMEM((2, width, hidden), BF), pltpu.VMEM((2, hidden, width), BF),
         pltpu.VMEM((2, width, third), BF), pltpu.VMEM((2, third, width), BF),
         pltpu.VMEM((2, width, 2 * width), BF), pltpu.VMEM((4, latents, width), F32),
         pltpu.VMEM((width, LANES), F32), pltpu.VMEM((2, hidden, LANES), F32),
         pltpu.VMEM((2, width + 8, hidden), F32), pltpu.VMEM((2, width, hidden), F32),
         pltpu.VMEM((2, width, third), F32), pltpu.VMEM((2, 8, width), F32),
         pltpu.VMEM((4, latents, width), F32), pltpu.VMEM((2, hidden, seq), BF),
         pltpu.VMEM((2, hidden, seq), BF)],
        grid=(own,), price=(8e9, 2e7))

    back_width = 2 * width
    tok_half, tok_whole, own_q, oth_q, rows_q, cond_own = local_call(
        functools.partial(back_kernel, dp, bits, rows), where,
        [tokens, condition, dx1, datt, qkv_act, prob, mods1, qkv_w, ada1, dact2],
        [tok_spec, full(condition.shape), col, half_col(third), half_col(3 * third), prob_spec,
         full(mods1.shape), full(qkv_w.shape), full(ada1.shape), full(dact2.shape)],
        [((T, width), BF), (tokens.shape, BF), ((dp, rows, back_width), BF),
         ((dp, rows, back_width), BF), ((latents, 2 * width), BF), ((latents, width), BF)],
        [flat, tok_spec, full((dp, rows, back_width)), full((dp, rows, back_width)),
         full((latents, 2 * width)), full((latents, width))],
        [pltpu.VMEM((2, width + 8, 3 * third), F32), pltpu.VMEM((2, latents, width), F32),
         pltpu.VMEM((2, 3 * third, seq), BF), pltpu.VMEM((2, width, LANES), F32)],
        grid=(own,), price=(6e9, 2e7))

    pairs = core_pairs(dp, mp)
    kept_m, came_m = reduced(own_m, oth_m, own_md, oth_md, bits, dp, mp)
    kept_q, came_q = reduced(own_q, oth_q, rows_q, rows_q, bits, dp, mp)
    condition_grad = (
        cond_own.astype(F32) + lax.ppermute(cond_own, AXES, pairs).astype(F32)).astype(BF)

    (widen_grad, narrow_grad, mix_grad, mix_b, narrow_b, widen_b, ada_m, ada_mb, act) = whole_call(
        functools.partial(last_mlp_kernel, rows, width), where, [kept_m, came_m],
        [((rows, hidden), F32), ((rows, hidden), F32), ((rows, third), F32), ((1, rows), F32),
         ((1, rows), F32), ((1, 2 * rows), F32), ((rows, 2 * width), F32), ((8, LANES), F32),
         ((LANES, dp * latents), BF)])
    qkv_grad, qv_b, adaln_weight_grad, adaln_bias_grad = whole_call(
        functools.partial(last_back_kernel, rows, width), where,
        [kept_q, came_q, act, ada_m, lax.ppermute(ada_m, AXES, pairs), ada_mb,
         lax.ppermute(ada_mb, AXES, pairs)],
        [((3, rows, third), F32), ((2, rows // 2), F32), ((rows, 6 * width), F32),
         ((6, rows), F32)])

    def joined(half, whole):
        came = lax.ppermute(half, AXES, pairs)
        return lax.dynamic_update_slice_in_dim(whole, came, (1 - core) * T, axis=0)

    return (
        joined(out_half, out_whole),
        joined(tok_half, tok_whole),
        condition_grad,
        adaln_weight_grad,
        adaln_bias_grad,
        qkv_grad,
        qv_b.reshape(2, 1, rows // 2),
        mix_grad.T,
        mix_b.reshape(rows),
        widen_grad,
        widen_b,
        narrow_grad.T,
        narrow_b.reshape(rows),
    )


def solution(mesh):
    return jax.shard_map(
        body,
        mesh=mesh,
        in_specs=(
            P("dp", None),
            P("dp", None),
            P("dp", None),
            P(None, "dp"),
            P(None, "dp", "mp"),
            P(None, "mp", "dp"),
            P("mp", "dp"),
            P("dp"),
            P("dp", "mp"),
            P("mp", "dp"),
            P("mp", "dp"),
            P("dp"),
            P("dp", None),
        ),
        out_specs=(
            P("dp", None),
            P("dp", None),
            P("dp", None),
            P("dp", None),
            P(None, "dp"),
            P(None, "dp", "mp"),
            P(None, "mp", "dp"),
            P("mp", "dp"),
            P("dp"),
            P("dp", "mp"),
            P("mp", "dp"),
            P("mp", "dp"),
            P("dp"),
        ),
        check_vma=False,
    )
```

```python
import functools

import jax
import jax.numpy as jnp
from jax import lax
from jax.experimental import pallas as pl
from jax.experimental.pallas import tpu as pltpu
from jax.sharding import PartitionSpec as P


HEAD_DIM = 64
EPS = 1e-06
BF = jnp.bfloat16
F32 = jnp.float32
AXES = ("dp", "mp")
GELU_A = 0.7978845608028654
GELU_B = 0.044715
BIAS = 64
LANES = 128
EXTRA = 16


def nn(a, b):
    return lax.dot_general(a, b, (((1,), (0,)), ((), ())), preferred_element_type=F32)


def nt(a, b):
    return lax.dot_general(a, b, (((1,), (1,)), ((), ())), preferred_element_type=F32)


def wide(column, tokens):
    return jnp.concatenate([column] * (tokens // LANES), axis=1)


def column_of(row):
    return jnp.broadcast_to(row, (LANES, row.shape[1])).T


def flipped(array):
    return array.astype(F32).T


def token_sum(array):
    return nt(jnp.ones((8, array.shape[1]), BF), array.astype(BF))


def normalized(x):
    mean = jnp.mean(x, axis=0, keepdims=True)
    centered = x - mean
    inverse = lax.rsqrt(jnp.mean(centered * centered, axis=0, keepdims=True) + EPS)
    return centered * inverse, inverse


def norm_back(grad, normed, inverse):
    first = jnp.mean(grad, axis=0, keepdims=True)
    second = jnp.mean(grad * normed, axis=0, keepdims=True)
    return (grad - first - normed * second) * inverse


def bit_orders(bits):
    down = list(range(bits - 1, -1, -1))
    other = down[:-2] + [down[-1], down[-2]] if bits > 1 else down
    return down, other


def place_of(apart, core, bits):
    orders = bit_orders(bits)
    places = [
        sum(((apart >> b) & 1) << p for p, b in enumerate(order)) for order in orders
    ]
    return jnp.where(core == 0, places[0], places[1])


def hop_pairs(phase, bits, dp, mp):
    orders = bit_orders(bits)
    return [
        (d * mp + c, (d ^ (1 << orders[c % 2][phase])) * mp + c)
        for d in range(dp)
        for c in range(mp)
    ]


def core_pairs(dp, mp):
    return [(d * mp + c, d * mp + (c ^ 1)) for d in range(dp) for c in range(mp)]


def pack_kernel(rows, adaln, adaln_b, qkv, qv_b, mix_t, mix_b, widen, widen_b, narrow_t,
                narrow_b, first_o, second_o, rows_s):
    core = lax.axis_index("mp")
    width = adaln.shape[1] // 6
    third, hidden = qkv.shape[2], widen.shape[1]
    half = rows // 2
    rows_s[...] = jnp.zeros_like(rows_s)
    rows_s[0:1, 0:half] = qv_b[0:1, :].astype(F32)
    rows_s[0:1, half:rows] = qv_b[1:2, :].astype(F32)
    rows_s[1:3, 0:rows] = adaln_b[0:2, :].astype(F32)
    rows_s[8:9, 0:rows] = widen_b[:, 0:rows].astype(F32)
    rows_s[9:10, 0:rows] = widen_b[:, rows : 2 * rows].astype(F32)
    rows_s[10:14, 0:rows] = adaln_b[2:6, :].astype(F32)
    rows_s[14:15, 0:rows] = mix_b[...].astype(F32)
    rows_s[15:16, 0:rows] = narrow_b[...].astype(F32)
    for out, at in ((first_o, 0), (second_o, 8)):
        turned = jnp.concatenate(
            [rows_s[at : at + 8, :], jnp.zeros((LANES - 8, LANES), F32)], axis=0).T
        out[:, out.shape[1] - BIAS :] = turned[0:rows, 0:BIAS].astype(BF)
    at = pl.multiple_of(core * width, LANES)
    first_o[:, 0:width] = adaln[:, pl.ds(at, width)]
    for j in range(3):
        first_o[:, width + j * third : width + (j + 1) * third] = qkv[j]
    at = pl.multiple_of((2 + 2 * core) * width, LANES)
    second_o[:, 0 : 2 * width] = adaln[:, pl.ds(at, 2 * width)]
    start = 2 * width
    second_o[:, start : start + hidden] = widen[...]
    second_o[:, start + hidden : start + 2 * hidden] = narrow_t[...]
    start += 2 * hidden
    second_o[:, start : start + third] = mix_t[...]


def gathered_blocks(where, dp, bits, mine, other):
    me, core = where[0], where[1]
    for parts, half in ((mine, core), (other, 1 - core)):
        for j in range(dp):
            at = place_of(me ^ j, half, bits)
            yield half, j, parts, at


def from_parts(parts, at, cut):
    low, high = parts
    count = low.shape[0]
    inside = lax.rem(at, count)
    return jnp.where(at < count, low[inside, :, cut], high[inside, :, cut])


def lane_only(block, lanes):
    keep = lax.broadcasted_iota(jnp.int32, block.shape, 1)
    return jnp.where(sum((keep == n).astype(jnp.int32) for n in lanes) > 0, block, 0.0)


def attention_kernel(dp, bits, rows, where, tok, cond, low, high, other_low, other_high,
                     att_o, qkv_o, prob_o, h1_o, qkv_w_o, ada_o, mod_o,
                     qkv_t, bias_s, plain_s):
    step = pl.program_id(0)
    core = where[1]
    seq, width = tok.shape
    third = qkv_o.shape[1] // 3
    heads = third // HEAD_DIM
    ones = jnp.ones((EXTRA, seq), BF)

    @pl.when(step == 0)
    def _():
        plain_s[...] = jnp.zeros_like(plain_s)
        for half, j, parts, at in gathered_blocks(
                where, dp, bits, (low, high), (other_low, other_high)):
            keep = slice(j * rows, (j + 1) * rows)
            ada_o[half, keep, :] = from_parts(parts, at, slice(0, width))
            qkv_w_o[half, keep, :] = from_parts(parts, at, slice(width, width + 3 * third))
            bias = from_parts(parts, at, slice(width + 3 * third, width + 3 * third + BIAS))
            bias = bias.astype(F32)
            bias_s[keep, 0:BIAS] = bias
            column = lane_only(bias, (0,))
            n = rows // 2
            plain_s[half, j * n : (j + 1) * n, 0:BIAS] = column[0:n]
            plain_s[half, 2 * third + j * n : 2 * third + (j + 1) * n, 0:BIAS] = column[n:]
        bias_rows = bias_s[...].T
        act = cond[...].astype(F32)
        act = (act * jax.nn.sigmoid(act)).astype(BF)
        for h in range(2):
            qkv_t[h, :, 0:width] = flipped(qkv_w_o[h]).astype(BF)
            qkv_t[h, :, width:] = plain_s[h].astype(BF)
            mod_o[h] = nn(act, ada_o[h]) + bias_rows[1 + h : 2 + h, :]

    row = core * pl.num_programs(0) + step
    shift = column_of(mod_o[0, pl.ds(row, 1), :])
    lift = 1.0 + column_of(mod_o[1, pl.ds(row, 1), :])
    normed, _ = normalized(flipped(tok[...]))
    h1 = (normed * wide(lift, seq) + wide(shift, seq)).astype(BF)
    h1_o[...] = h1
    h1 = jnp.concatenate([h1, ones], axis=0)
    for h in range(2):
        qkv_o[h] = nn(qkv_t[h, :, 0 : width + EXTRA], h1).astype(BF)

    def scores_of(n):
        h, base = divmod(n, heads)
        base *= HEAD_DIM
        q = qkv_o[h, base : base + HEAD_DIM, :]
        k = qkv_o[h, third + base : third + base + HEAD_DIM, :]
        keys = flipped(k).astype(BF)
        return nn(keys, (q.astype(F32) * HEAD_DIM**-0.5).astype(BF))

    def finish(n, scores):
        h, base = divmod(n, heads)
        base *= HEAD_DIM
        v = qkv_o[h, 2 * third + base : 2 * third + base + HEAD_DIM, :]
        top = jnp.max(scores, axis=0, keepdims=True)
        raised = jnp.exp(scores - top)
        prob = (raised * (1.0 / jnp.sum(raised, axis=0, keepdims=True))).astype(BF)
        prob_o[n] = prob
        att_o[h, base : base + HEAD_DIM, :] = nn(v, prob).astype(BF)

    held = scores_of(0)
    for n in range(2 * heads):
        ahead = scores_of(n + 1) if n + 1 < 2 * heads else None
        finish(n, held)
        held = ahead


def put_blocks(dp, bits, where, outs, make):
    me, core = where[0], where[1]
    for out, half in zip(outs, (core, 1 - core)):
        for j in range(dp):
            out[place_of(me ^ j, half, bits)] = make(half, j).astype(BF)


def mlp_kernel(dp, bits, rows, where, tok, cot, att, cond, low, high, other_low, other_high,
               out_o, whole_o, datt_o, dx1_o, own_o, oth_o, own_d, oth_d, dact_o,
               widen_t, widen, narrow_t, narrow, mix_t, mix, ada, mods, bias_s, plain_s,
               w_acc, n_acc, m_acc, sums, dmods, g_s, du_s):
    step = pl.program_id(0)
    core = where[1]
    seq, width = cot.shape
    hidden = widen.shape[2]
    ones = jnp.ones((EXTRA, seq), BF)

    @pl.when(step == 0)
    def _():
        w_acc[...] = jnp.zeros_like(w_acc)
        n_acc[...] = jnp.zeros_like(n_acc)
        m_acc[...] = jnp.zeros_like(m_acc)
        sums[...] = jnp.zeros_like(sums)
        dmods[...] = jnp.zeros_like(dmods)
        plain_s[...] = jnp.zeros_like(plain_s)
        for half, j, parts, at in gathered_blocks(
                where, dp, bits, (low, high), (other_low, other_high)):
            keep = slice(j * rows, (j + 1) * rows)
            start = 0
            for ref in (ada, widen, narrow_t, mix_t):
                n = ref.shape[2]
                ref[half, keep, :] = from_parts(parts, at, slice(start, start + n))
                start += n
            bias = from_parts(parts, at, slice(start, start + BIAS)).astype(F32)
            bias_s[keep, 0:BIAS] = bias
            at = 2 * rows * j
            plain_s[half, at : at + rows, 0:BIAS] = lane_only(bias, (0,))
            plain_s[half, at + rows : at + 2 * rows, 0:BIAS] = lane_only(bias, (1,))
        bias_rows = bias_s[...].T
        act = cond[...].astype(F32)
        act = (act * jax.nn.sigmoid(act)).astype(BF)
        for h in range(2):
            widen_t[h, :, 0:width] = flipped(widen[h]).astype(BF)
            widen_t[h, :, width:] = plain_s[h].astype(BF)
            narrow[h] = flipped(narrow_t[h]).astype(BF)
            mix[h] = flipped(mix_t[h]).astype(BF)
            found = nn(act, ada[h])
            for p in range(2):
                n = 2 * h + p
                mods[n] = found[:, p * width : (p + 1) * width] + bias_rows[2 + n : 3 + n, :]

    row = core * pl.num_programs(0) + step
    gate1, shift2, scale2, gate2 = (
        wide(column_of(mods[n, pl.ds(row, 1), :]), seq) for n in range(4))
    abr = nn(mix_t[0], att[0]) + nn(mix_t[1], att[1])
    abr = abr + jnp.broadcast_to(bias_s[:, 6:7], abr.shape)
    x1 = flipped(tok[...]) + gate1 * abr
    normed, inverse = normalized(x1)
    lift = 1.0 + scale2
    h2 = (normed * lift + shift2).astype(BF)
    h2 = jnp.concatenate([h2, ones], axis=0)
    dy = flipped(cot[...])
    dm = (gate2 * dy).astype(BF)
    chunk = 256 if hidden % 256 == 0 else hidden
    cuts = [(h, slice(at, at + chunk)) for h in range(2) for at in range(0, hidden, chunk)]

    def grads(h, cut):
        n_acc[h, :, cut] += nt(dm, g_s[h, cut, :])
        w_acc[h, :, cut] += nt(h2[0 : width + 8], du_s[h, cut, :])

    def opened(h, cut):
        return nn(widen_t[h, cut, 0 : width + EXTRA], h2), nn(narrow[h, cut, :], dm)

    held = opened(*cuts[0])
    for n, (h, cut) in enumerate(cuts):
        u, dg = held
        if n + 1 < len(cuts):
            held = opened(*cuts[n + 1])
        if n > 0:
            grads(*cuts[n - 1])
        squared = u * u
        part = 0.5 * jnp.tanh(u * (GELU_A + (GELU_A * GELU_B) * squared)) + 0.5
        g = u * part
        slope = part + (g - g * part) * (2 * GELU_A + (6 * GELU_A * GELU_B) * squared)
        g_s[h, cut, :] = g.astype(BF)
        du_s[h, cut, :] = (dg * slope).astype(BF)
    grads(*cuts[-1])
    mbr = nn(narrow_t[0], g_s[0]) + nn(narrow_t[1], g_s[1])
    dh2 = nn(widen[0], du_s[0]) + nn(widen[1], du_s[1])
    mbr = mbr + jnp.broadcast_to(bias_s[:, 7:8], mbr.shape)
    y = (x1 + gate2 * mbr).T.astype(BF)
    out_o[...] = y
    whole_o[...] = y
    dx1 = dy + norm_back(dh2 * lift, normed, inverse)
    dx1_o[...] = dx1
    da = (gate1 * dx1).astype(BF)
    for h in range(2):
        m_acc[h] += nt(da, att[h])
        datt_o[h] = nn(mix[h], da).astype(BF)
    sums[0] += token_sum(da)
    sums[1] += token_sum(dm)
    for n, found in enumerate((dx1 * abr, dh2, dh2 * normed, dy * mbr)):
        dmods[n, pl.ds(row, 1), :] = token_sum(found)[0:1]

    @pl.when(step == pl.num_programs(0) - 1)
    def _():
        turned = [w_acc[h, width : width + 8, :].T for h in range(2)]
        flat = [sums[n].T for n in range(2)]
        for h in range(2):
            for j in range(dp):
                at = 2 * rows * j
                keep = slice(j * rows, (j + 1) * rows)
                cols = [flat[0][keep, 0:1], flat[1][keep, 0:1],
                        turned[h][at : at + rows, 0:1], turned[h][at + rows : at + 2 * rows, 0:1]]
                lane = lax.broadcasted_iota(jnp.int32, (rows, BIAS), 1)
                block = jnp.zeros((rows, BIAS), F32)
                for n, c in enumerate(cols):
                    block = jnp.where(lane == n, jnp.broadcast_to(c, block.shape), block)
                plain_s[h, keep, 0:BIAS] = block

        def make(half, j):
            keep = slice(j * rows, (j + 1) * rows)
            return jnp.concatenate(
                [w_acc[half, keep, :], n_acc[half, keep, :], m_acc[half, keep, :],
                 plain_s[half, keep, 0:BIAS]], axis=1)

        put_blocks(dp, bits, where, (own_o, oth_o), make)
        act = cond[...].astype(F32)
        act = act * jax.nn.sigmoid(act)
        mine = lax.broadcasted_iota(jnp.int32, act.shape, 0) // pl.num_programs(0) == core
        act = jnp.where(mine, act, 0.0).astype(BF)
        dact = jnp.zeros(act.shape, F32)
        for n in range(4):
            dact = dact + nt(dmods[n].astype(BF), ada[n // 2, :, (n % 2) * width : (n % 2 + 1) * width])
        dact_o[...] = dact
        for out, half in ((own_d, core), (oth_d, 1 - core)):
            for p in range(2):
                out[:, p * width : (p + 1) * width] = dmods[2 * half + p].astype(BF)
            out[:, 2 * width : 3 * width] = act


def back_kernel(start, own, where, tok, dx1_r, datt, qkv, prob_r, mods, qkv_w, *rest):
    dqkv, sums_o, tok_o, whole_o = rest[-4:]
    step = pl.program_id(0)
    core = where[1]
    seq, _ = tok.shape
    third = qkv.shape[1] // 3
    heads = third // HEAD_DIM
    row = core * own + start + step
    lift = 1.0 + wide(column_of(mods[1, pl.ds(row, 1), :]), seq)

    def dprob_of(n):
        h, base = divmod(n, heads)
        base *= HEAD_DIM
        v = qkv[h, 2 * third + base : 2 * third + base + HEAD_DIM, :]
        return nn(flipped(v).astype(BF), datt[h, base : base + HEAD_DIM, :])

    def finish(n, dprob):
        h, base = divmod(n, heads)
        base *= HEAD_DIM
        q = qkv[h, base : base + HEAD_DIM, :]
        k = qkv[h, third + base : third + base + HEAD_DIM, :]
        prob = prob_r[n]
        prob_f = prob.astype(F32)
        weighted = prob_f * dprob
        inner = jnp.sum(weighted, axis=0, keepdims=True)
        dscores = (weighted - prob_f * inner).astype(BF)
        dqkv[h, base : base + HEAD_DIM, :] = (nn(k, dscores) * HEAD_DIM**-0.5).astype(BF)
        dqkv[h, third + base : third + base + HEAD_DIM, :] = (
            nt(q, dscores) * HEAD_DIM**-0.5).astype(BF)
        dqkv[h, 2 * third + base : 2 * third + base + HEAD_DIM, :] = nt(
            datt[h, base : base + HEAD_DIM, :], prob).astype(BF)

    held = dprob_of(0)
    for n in range(2 * heads):
        ahead = dprob_of(n + 1) if n + 1 < 2 * heads else None
        finish(n, held)
        held = ahead
    normed, inverse = normalized(flipped(tok[...]))
    dh1 = nn(qkv_w[0], dqkv[0]) + nn(qkv_w[1], dqkv[1])
    grad = dx1_r[...] + norm_back(dh1 * lift, normed, inverse)
    grad = grad.T.astype(BF)
    tok_o[...] = grad
    whole_o[...] = grad
    for n, found in enumerate((dh1, dh1 * normed)):
        sums_o[0, n] = token_sum(found)


def grads_kernel(dp, bits, rows, own, calls, where, cond, h1, ada, dact2, *rest):
    dqkv, sums = rest[:calls], rest[calls : 2 * calls]
    own_o, oth_o, rows_o, cond_o, q_acc, dmods, plain_s = rest[2 * calls :]
    core = where[1]
    width = h1.shape[0]
    third = dqkv[0].shape[1] // 3
    every = h1.shape[1]
    left = jnp.concatenate([h1[...], jnp.ones((8, every), BF)], axis=0)
    n = rows // 2
    for h in range(2):
        right = jnp.concatenate([d[h] for d in dqkv], axis=1)
        q_acc[h] = nt(left, right)
        turned = q_acc[h, width : width + 8, :].T
        for j in range(dp):
            for at, start in ((0, 0), (n, 2 * third)):
                plain_s[h, j * rows + at : j * rows + at + n, :] = jnp.broadcast_to(
                    turned[start + j * n : start + (j + 1) * n, 0:1], (n, LANES))

    def make(half, j):
        keep = slice(j * rows, (j + 1) * rows)
        return jnp.concatenate(
            [q_acc[half, keep, :], plain_s[half, keep, 0:BIAS],
             jnp.zeros((rows, own_o.shape[2] - 3 * third - BIAS), F32)], axis=1)

    put_blocks(dp, bits, where, (own_o, oth_o), make)
    dmods[...] = jnp.zeros_like(dmods)
    at = 0
    for part in sums:
        for i in range(part.shape[0]):
            for p in range(2):
                dmods[p, pl.ds(core * own + at, 1), :] = part[i, p, 0:1, :]
            at += 1
    c = cond[...].astype(F32)
    s = jax.nn.sigmoid(c)
    dact = dact2[...]
    for p in range(2):
        dact = dact + nt(dmods[p].astype(BF), ada[p])
    cond_o[...] = (dact * (s + c * s * (1.0 - s))).astype(BF)
    for p in range(2):
        rows_o[:, p * width : (p + 1) * width] = dmods[p].astype(BF)


def apart_of(place, bits):
    order = bit_orders(bits)[0]
    return sum(((place >> p) & 1) << b for p, b in enumerate(order))


def picked(me, rows, width, count, bits):
    lane = lax.broadcasted_iota(jnp.int32, (1, LANES), 1)
    wanted = jnp.full((1, LANES), -1, jnp.int32)
    for k in range(count):
        inside = lane - k * rows
        target = rows * (me ^ apart_of(k, bits)) + inside
        wanted = jnp.where(jnp.where(inside >= 0, inside, rows) < rows, target, wanted)
    feature = lax.broadcasted_iota(jnp.int32, (width, LANES), 0)
    return (feature == jnp.broadcast_to(wanted, feature.shape)).astype(F32).astype(BF)


def open_kernel(own, got, own_rows, got_rows, out):
    count, rows = own.shape[0], own.shape[1]
    half = count // 2
    for k in range(half):
        both = own[half + k].astype(F32) + got[half + k].astype(F32)
        out[k * rows : (k + 1) * rows, :] = both.astype(BF)
    both = (own_rows[...].astype(F32) + got_rows[...].astype(F32)).astype(BF)
    n = own_rows.shape[0]
    out[half * rows :, 0 : both.shape[1]] = both
    if both.shape[1] < out.shape[1]:
        out[half * rows :, both.shape[1] :] = jnp.zeros((n, out.shape[1] - both.shape[1]), BF)


def second_kernel(own, got, sent, came, kept_o, out):
    count, rows = own.shape[0], own.shape[1]
    half, quarter = count // 2, count // 4
    for k in range(half):
        cut = slice(k * rows, (k + 1) * rows)
        total = own[k].astype(F32) + got[k].astype(F32) + came[cut, :].astype(F32)
        if k < quarter:
            kept_o[cut, :] = total
        else:
            out[(k - quarter) * rows : (k - quarter + 1) * rows, :] = total.astype(BF)
    n = came.shape[0] - half * rows
    out[quarter * rows : quarter * rows + n, :] = sent[half * rows :, :]
    out[quarter * rows + n :, :] = came[half * rows :, :]


def middle_kernel(rows, width, bits, first_lane, pieces, used, *refs):
    if pieces[1] is None:
        kept, sent, came, act_in, kept_o, out = refs
        me = lax.axis_index("dp")
    else:
        kept, sent, came, kept_o, out, act_in = refs
        me = lax.axis_index("dp")
    count = kept.shape[0]
    near = count // 2
    total = kept[...] + came[0:count, :].astype(F32)
    every = jnp.concatenate([sent[count:, :], came[count:, :]], axis=0)
    pick = picked(me, rows, width, count // rows, bits)
    columns = pieces[0] * width
    if pieces[1] is not None:
        act = nn(every[:, pieces[1] * width : (pieces[1] + 1) * width], pick).T.astype(BF)
        act_in[...] = act
    else:
        act = act_in[...]
    ada = nn(act, every[:, 0:columns])[0:count]
    lane = lax.broadcasted_iota(jnp.int32, (8, LANES), 0)
    sums = jnp.zeros((8, LANES), F32)
    for p in range(pieces[0]):
        found = nn(every[:, p * width : (p + 1) * width], pick)
        sums = jnp.where(lane == p, jnp.sum(found, axis=0, keepdims=True), sums)
    turned = sums.T[0:count]
    small = total[:, used - BIAS : used]
    lane = lax.broadcasted_iota(jnp.int32, small.shape, 1)
    for p in range(pieces[0]):
        small = jnp.where(lane == first_lane + p, jnp.broadcast_to(turned[:, p : p + 1], small.shape), small)
    joined = jnp.concatenate([total[:, 0 : used - BIAS], small, ada], axis=1)
    kept_o[...] = joined[0:near]
    out[...] = joined[near:].astype(BF)


def step_kernel(kept, came, kept_o, out):
    near = kept.shape[0] // 2
    kept_o[...] = kept[0:near] + came[0:near, :].astype(F32)
    out[...] = (kept[near:] + came[near:, :].astype(F32)).astype(BF)


def last_mlp_kernel(rows, hidden, third, kept, came, widen_o, narrow_o, mix_o, mix_b, narrow_b,
                    widen_b, ada_o, ada_b):
    total = kept[...] + came[...].astype(F32)
    widen_o[...] = total[:, 0:hidden]
    narrow_o[...] = total[:, hidden : 2 * hidden]
    mix_o[...] = total[:, 2 * hidden : 2 * hidden + third]
    start = 2 * hidden + third
    small = total[:, start : start + BIAS].T
    mix_b[...] = small[0:1, :]
    narrow_b[...] = small[1:2, :]
    widen_b[:, 0:rows] = small[2:3, :]
    widen_b[:, rows : 2 * rows] = small[3:4, :]
    ada_o[...] = total[:, start + BIAS :]
    ada_b[...] = jnp.zeros_like(ada_b)
    ada_b[0:2, 0:rows] = small[4:6, :]


def last_back_kernel(rows, width, kept, came, early, early_other, early_b, early_other_b, qkv_o, qv_b,
                     ada_o, ada_b):
    third = qkv_o.shape[2]
    core = lax.axis_index("mp")
    total = kept[...] + came[...].astype(F32)
    for j in range(3):
        qkv_o[j] = total[:, j * third : (j + 1) * third]
    small = total[:, 3 * third : 3 * third + BIAS].T
    n = rows // 2
    qv_b[0:1, :] = small[0:1, 0:n]
    qv_b[1:2, :] = small[0:1, n:rows]
    ada_o[:, 0 : 2 * width] = total[:, 3 * third + BIAS :]
    ada_b[0:2, :] = small[1:3, :]
    for half, values in ((core, early), (1 - core, early_other)):
        at = pl.multiple_of((2 + 2 * half) * width, LANES)
        ada_o[:, pl.ds(at, 2 * width)] = values[...]
    first = jnp.where(core == 0, early_b[...], early_other_b[...])
    second = jnp.where(core == 0, early_other_b[...], early_b[...])
    ada_b[2:4, :] = first[0:2, 0:rows]
    ada_b[4:6, :] = second[0:2, 0:rows]


def full(shape):
    return pl.BlockSpec(tuple(shape), lambda *_: (0,) * len(shape))


def cost(flops, nbytes):
    return pl.CostEstimate(flops=int(flops), bytes_accessed=int(nbytes), transcendentals=0)


MIB = {"pack": 58, "attention": 20, "mlp": 40, "back": 16}


def params_of(name):
    return pltpu.CompilerParams(vmem_limit_bytes=MIB.get(name.rstrip("0123456789"), 12) << 20)


def local_call(kernel, where, args, in_specs, outs, out_specs, scratch=(), grid=(1,), price=(1e6, 4e6),
               name=None, aliases=None):
    return pl.pallas_call(
        kernel,
        out_shape=[jax.ShapeDtypeStruct(tuple(s), d) for s, d in outs],
        grid_spec=pltpu.PrefetchScalarGridSpec(
            num_scalar_prefetch=1, grid=grid, in_specs=in_specs, out_specs=out_specs,
            scratch_shapes=list(scratch)),
        compiler_params=params_of(name),
        cost_estimate=cost(*price),
        input_output_aliases=aliases or {},
    )(where, *args)


def plain_call(kernel, args, outs, scratch=(), name=None):
    return pl.pallas_call(
        kernel,
        out_shape=[jax.ShapeDtypeStruct(tuple(s), d) for s, d in outs],
        in_specs=[pl.BlockSpec(memory_space=pltpu.VMEM)] * len(args),
        out_specs=[pl.BlockSpec(memory_space=pltpu.VMEM)] * len(outs),
        scratch_shapes=list(scratch),
        compiler_params=params_of(name),
        cost_estimate=cost(1e6, 1e6),
    )(*args)


def whole_call(kernel, where, args, outs, scratch=(), name=None):
    return local_call(kernel, where, args, [full(a.shape) for a in args], outs,
                      [full(s) for s, _ in outs], scratch, name=name)


def hop(array, pairs):
    return lax.ppermute(array, AXES, pairs)


def join_kernel(low, high, out):
    n = low.shape[0]
    out[0:n] = low[...]
    out[n : 2 * n] = high[...]


def gathered(message, bits, dp, mp, tag):
    held = message[None]
    came = None
    for phase in range(bits):
        if came is not None:
            shape = (2 * held.shape[0], *held.shape[1:])
            held, = plain_call(join_kernel, [held, came], [(shape, BF)], name=f"{tag}join{phase}")
        came = hop(held, hop_pairs(phase, bits, dp, mp))
    pairs = core_pairs(dp, mp)
    return held, came, hop(held, pairs), hop(came, pairs)


def reduced(own, other, own_rows, other_rows, bits, dp, mp, tag, width, used, first_lane, pieces, act=None):
    rows, wide_by = own.shape[1:]
    pairs = core_pairs(dp, mp)
    got = hop(other, pairs)
    got_rows = hop(other_rows, pairs)
    extra = own_rows.shape[0]
    n = dp // 2 * rows
    sent, = plain_call(open_kernel, [own, got, own_rows, got_rows], [((n + extra, wide_by), BF)],
                       name=f"{tag}open")
    came = hop(sent, hop_pairs(bits - 1, bits, dp, mp))
    n //= 2
    kept, sent = plain_call(second_kernel, [own, got, sent, came],
                            [((n, wide_by), F32), ((n + 2 * extra, wide_by), BF)], name=f"{tag}second")
    came = hop(sent, hop_pairs(bits - 2, bits, dp, mp))
    columns = used + pieces[0] * width
    outs = [((n // 2, columns), F32), ((n // 2, columns), BF)]
    ins = [kept, sent, came]
    if act is None:
        outs.append(((LANES, 4 * extra), BF))
    else:
        ins.append(act)
    kept, sent, *acts = plain_call(
        functools.partial(middle_kernel, rows, width, bits, first_lane, pieces, used), ins, outs,
        name=f"{tag}middle")
    for phase in reversed(range(bits - 2)):
        came = hop(sent, hop_pairs(phase, bits, dp, mp))
        if phase:
            n = kept.shape[0] // 2
            kept, sent = plain_call(step_kernel, [kept, came], [((n, columns), F32), ((n, columns), BF)],
                                    name=f"{tag}step{phase}")
    return kept, came, acts


def body(
    tokens,
    condition,
    adaln_weight,
    adaln_bias,
    qkv_weight,
    qv_bias,
    mix_weight,
    mix_bias,
    widen_weight,
    widen_bias,
    narrow_weight,
    narrow_bias,
    cotangent,
):
    dp, mp = lax.axis_size("dp"), lax.axis_size("mp")
    bits = dp.bit_length() - 1
    me, core = lax.axis_index("dp"), lax.axis_index("mp")
    latents = condition.shape[0]
    own = latents // mp
    seq = tokens.shape[0] // latents
    width = tokens.shape[1]
    rows = width // dp
    third = qkv_weight.shape[2]
    hidden = widen_weight.shape[1]
    where = jnp.stack([me, core]).astype(jnp.int32)
    T = own * seq
    heads = 2 * third // HEAD_DIM

    first_width = width + 3 * third + BIAS
    second_width = 2 * width + 2 * hidden + third + BIAS
    first, second = plain_call(
        functools.partial(pack_kernel, rows),
        [adaln_weight, adaln_bias, qkv_weight, qv_bias.reshape(2, rows // 2), mix_weight.T,
         mix_bias.reshape(1, rows), widen_weight, widen_bias, narrow_weight.T,
         narrow_bias.reshape(1, rows)],
        [((rows, first_width), BF), ((rows, second_width), BF)],
        [pltpu.VMEM((16, LANES), F32)], name="pack")

    part_a = gathered(first, bits, dp, mp, "a")
    part_b = gathered(second, bits, dp, mp, "b")

    tok_spec = pl.BlockSpec((seq, width), lambda i, w: (w[1] * own + i, 0))
    col = pl.BlockSpec((width, seq), lambda i, w: (0, i))
    half_col = lambda n: pl.BlockSpec((2, n, seq), lambda i, w: (0, 0, i))
    prob_spec = pl.BlockSpec((heads, seq, seq), lambda i, w: (i, 0, 0))
    flat = pl.BlockSpec((seq, width), lambda i, w: (i, 0))

    def fulls(arrays):
        return [full(a.shape) for a in arrays]

    att, qkv_act, prob, h1, qkv_w, ada1, mods1 = local_call(
        functools.partial(attention_kernel, dp, bits, rows), where,
        [tokens, condition, *part_a],
        [tok_spec, full(condition.shape), *fulls(part_a)],
        [((2, third, T), BF), ((2, 3 * third, T), BF), ((own * heads, seq, seq), BF),
         ((width, T), BF), ((2, width, 3 * third), BF), ((2, width, width), BF), ((2, latents, width), F32)],
        [half_col(third), half_col(3 * third), prob_spec, col, full((2, width, 3 * third)),
         full((2, width, width)), full((2, latents, width))],
        [pltpu.VMEM((2, 3 * third, width + LANES), BF), pltpu.VMEM((width, LANES), F32),
         pltpu.VMEM((2, 3 * third, LANES), F32)],
        grid=(own,), price=(3e9, 2e7), name="attention")

    send_width = 2 * hidden + third + BIAS
    out_half, out_whole, datt, dx1, own_m, oth_m, own_md, oth_md, dact2 = local_call(
        functools.partial(mlp_kernel, dp, bits, rows), where,
        [tokens, cotangent, att, condition, *part_b],
        [tok_spec, tok_spec, half_col(third), full(condition.shape), *fulls(part_b)],
        [((T, width), BF), (tokens.shape, BF), ((2, third, T), BF), ((width, T), F32),
         ((dp, rows, send_width), BF), ((dp, rows, send_width), BF),
         ((latents, 3 * width), BF), ((latents, 3 * width), BF), ((latents, width), F32)],
        [flat, tok_spec, half_col(third), col, full((dp, rows, send_width)),
         full((dp, rows, send_width)), full((latents, 3 * width)), full((latents, 3 * width)),
         full((latents, width))],
        [pltpu.VMEM((2, hidden, width + LANES), BF), pltpu.VMEM((2, width, hidden), BF),
         pltpu.VMEM((2, width, hidden), BF), pltpu.VMEM((2, hidden, width), BF),
         pltpu.VMEM((2, width, third), BF), pltpu.VMEM((2, third, width), BF),
         pltpu.VMEM((2, width, 2 * width), BF), pltpu.VMEM((4, latents, width), F32),
         pltpu.VMEM((width, LANES), F32), pltpu.VMEM((2, hidden, LANES), F32),
         pltpu.VMEM((2, width + 8, hidden), F32), pltpu.VMEM((2, width, hidden), F32),
         pltpu.VMEM((2, width, third), F32), pltpu.VMEM((2, 8, width), F32),
         pltpu.VMEM((4, latents, width), F32), pltpu.VMEM((2, hidden, seq), BF),
         pltpu.VMEM((2, hidden, seq), BF)],
        grid=(own,), price=(8e9, 2e7), name="mlp")

    back_width = 2 * width
    splits = [1, own - 1] if own > 1 else [own]
    dqkv, sums, halves, whole, at = [], [], None, None, 0
    for number, count in enumerate(splits):
        first_at = at
        tok_at = pl.BlockSpec((seq, width), lambda i, w, s=first_at: (w[1] * own + s + i, 0))
        ins = [tokens, dx1, datt, qkv_act, prob, mods1, qkv_w]
        in_specs = [
            tok_at, pl.BlockSpec((width, seq), lambda i, w, s=first_at: (0, i + s)),
            *(pl.BlockSpec((2, n, seq), lambda i, w, s=first_at: (0, 0, i + s))
              for n in (third, 3 * third)),
            pl.BlockSpec((heads, seq, seq), lambda i, w, s=first_at: (i + s, 0, 0)),
            full(mods1.shape), full(qkv_w.shape)]
        aliases = {}
        if whole is not None:
            aliases = {1 + len(ins): 2, 2 + len(ins): 3}
            ins += [halves, whole]
            in_specs += [pl.BlockSpec(memory_space=pl.ANY)] * 2
        d, s_rows, halves, whole = local_call(
            functools.partial(back_kernel, at, own), where, ins, in_specs,
            [((2, 3 * third, count * seq), BF), ((count, 2, 8, width), F32),
             ((T, width), BF), (tokens.shape, BF)],
            [half_col(3 * third), pl.BlockSpec((1, 2, 8, width), lambda i, w: (i, 0, 0, 0)),
             pl.BlockSpec((seq, width), lambda i, w, s=first_at: (i + s, 0)), tok_at],
            grid=(count,), price=(1.5e9 * count, 5e6), name=f"back{number}", aliases=aliases)
        dqkv.append(d)
        sums.append(s_rows)
        at += count
    tok_whole = whole
    own_q, oth_q, rows_q, cond_own = whole_call(
        functools.partial(grads_kernel, dp, bits, rows, own, len(splits)), where,
        [condition, h1, ada1, dact2, *dqkv, *sums],
        [((dp, rows, back_width), BF), ((dp, rows, back_width), BF), ((latents, 2 * width), BF),
         ((latents, width), BF)],
        [pltpu.VMEM((2, width + 8, 3 * third), F32), pltpu.VMEM((2, latents, width), F32),
         pltpu.VMEM((2, width, LANES), F32)], name="grads")

    pairs = core_pairs(dp, mp)
    kept_m, came_m, (act,) = reduced(
        own_m, oth_m, own_md, oth_md, bits, dp, mp, "m", width, send_width, 4, (2, 2))
    kept_q, came_q, _ = reduced(
        own_q, oth_q, rows_q, rows_q, bits, dp, mp, "q", width, 3 * third + BIAS, 1, (2, None), act)
    condition_grad = (
        cond_own.astype(F32) + lax.ppermute(cond_own, AXES, pairs).astype(F32)).astype(BF)

    (widen_grad, narrow_grad, mix_grad, mix_b, narrow_b, widen_b, ada_m, ada_mb) = plain_call(
        functools.partial(last_mlp_kernel, rows, hidden, third), [kept_m, came_m],
        [((rows, hidden), F32), ((rows, hidden), F32), ((rows, third), F32), ((1, rows), F32),
         ((1, rows), F32), ((1, 2 * rows), F32), ((rows, 2 * width), F32), ((8, LANES), F32)],
        name="last_mlp")
    qkv_grad, qv_b, adaln_weight_grad, adaln_bias_grad = plain_call(
        functools.partial(last_back_kernel, rows, width),
        [kept_q, came_q, ada_m, lax.ppermute(ada_m, AXES, pairs), ada_mb,
         lax.ppermute(ada_mb, AXES, pairs)],
        [((3, rows, third), F32), ((2, rows // 2), F32), ((rows, 6 * width), F32),
         ((6, rows), F32)],
        name="last_back")

    def joined(half, whole):
        came = hop(half, pairs)
        return lax.dynamic_update_slice_in_dim(whole, came, (1 - core) * T, axis=0)

    return (
        joined(out_half, out_whole),
        joined(halves, tok_whole),
        condition_grad,
        adaln_weight_grad,
        adaln_bias_grad,
        qkv_grad,
        qv_b.reshape(2, 1, rows // 2),
        mix_grad.T,
        mix_b.reshape(rows),
        widen_grad,
        widen_b,
        narrow_grad.T,
        narrow_b.reshape(rows),
    )


def solution(mesh):
    return jax.shard_map(
        body,
        mesh=mesh,
        in_specs=(
            P("dp", None),
            P("dp", None),
            P("dp", None),
            P(None, "dp"),
            P(None, "dp", "mp"),
            P(None, "mp", "dp"),
            P("mp", "dp"),
            P("dp"),
            P("dp", "mp"),
            P("mp", "dp"),
            P("mp", "dp"),
            P("dp"),
            P("dp", None),
        ),
        out_specs=(
            P("dp", None),
            P("dp", None),
            P("dp", None),
            P("dp", None),
            P(None, "dp"),
            P(None, "dp", "mp"),
            P(None, "mp", "dp"),
            P("mp", "dp"),
            P("dp"),
            P("dp", "mp"),
            P("mp", "dp"),
            P("mp", "dp"),
            P("dp"),
        ),
        check_vma=False,
    )
```
